32 devices in a mesh: groups: 2 (over x), dp: 8 (over z, y), tensor: 2 (over core).
Axes of the slice: x: 2, y: 2, z: 4, core: 2. Of those that a mesh axis runs over, the one named last changes fastest.
Arguments:
- queries: bfloat16 [4096, 4096], P(('groups', 'dp'), 'tensor'), parts along dimension 0, may hold values from -6.5 to 6.5
- fresh_keys: bfloat16 [4096, 512], P(('groups', 'dp'), 'tensor'), parts along dimension 0, may hold values from -4 to 4
- fresh_values: bfloat16 [4096, 512], P(('groups', 'dp'), 'tensor'), parts along dimension 0, may hold values from -4 to 4
- key_pool_pages: bfloat16 [160, 128, 512], P(('groups', 'dp'), None, 'tensor'), parts along dimension 0, may hold values from -4 to 4
- value_pool_pages: bfloat16 [160, 128, 512], P(('groups', 'dp'), None, 'tensor'), parts along dimension 0, may hold values from -4 to 4
- block_table: int32 [16, 8], P(('groups', 'dp')), parts along dimension 0, may hold values from 0 to 9, as said below
- prefix_lengths: int32 [16], P('groups'), parts along dimension 0, may hold values from 0 to 1024, as said below
- out_weight: bfloat16 [4096, 4096], P('tensor', 'dp'), may hold values from -0.09375 to 0.09375
Outputs:
- output: bfloat16 [4096, 4096], P(('groups', 'dp'), 'tensor'), parts along dimension 0
The draws below stay inside these ranges and needn't reach their ends.
There are 2 independent parts, one for each index of `groups`. The reference program is written for one: setup_inputs(seed, part) draws one part's arguments, and reference() takes and returns one part's arrays. A program takes and returns all parts, laid end to end along the dimension named above; an argument that names none is the same for every part. Nothing has to cross between parts.
Inputs may be any that keep to these rules, and one draw needn't show every extreme that they name: `block_table`: each row holds distinct pages of the request's own pool of 10 pages. `prefix_lengths`: some request has exactly 1024 cached tokens and some has none.
All inputs are finite; a program needn't handle non-finite values.
Results may differ from the reference program's by a relative error of at most 0.0095.
Values may be sent and summed in bfloat16 or wider, within the bound.
A program may use at most 128 MiB of HBM per device.

```python
import jax
import jax.numpy as jnp
from jax import lax

D = 4096
HEAD_SIZE = 128
KEY_VALUE_HEADS = 4
QUERY_GROUP = 8
HQ = 32
REQUEST_TOKENS = 256
PAGE_TOKENS = 128
PAGES = 8
MAX_CACHED = 1024
POOL_PAGES = 10
REQUEST_COUNT = 8
ALL_TOKENS = 2048


def draw_queries(key, part):
    window_width = HQ * HEAD_SIZE
    base_random_draw = jnp.clip(jax.random.normal(jax.random.fold_in(key, 11), (REQUEST_COUNT, REQUEST_TOKENS, window_width), jnp.float32), -4.0, 4.0)
    return base_random_draw.reshape(ALL_TOKENS, window_width).astype(jnp.bfloat16)


def draw_fresh_keys(key, part):
    window_width = KEY_VALUE_HEADS * HEAD_SIZE
    base_random_draw = jnp.clip(jax.random.normal(jax.random.fold_in(key, 13), (REQUEST_COUNT, REQUEST_TOKENS, window_width), jnp.float32), -4.0, 4.0)
    return base_random_draw.reshape(ALL_TOKENS, window_width).astype(jnp.bfloat16)


def draw_prefix_lengths(key, part):
    first_draw = jax.random.randint(jax.random.fold_in(key, 21), (REQUEST_COUNT,), 0, MAX_CACHED + 1)
    second_draw = jax.random.randint(jax.random.fold_in(key, 22), (REQUEST_COUNT,), 0, MAX_CACHED + 1)
    lengths = first_draw * second_draw // MAX_CACHED
    chosen = jax.random.randint(jax.random.fold_in(key, 23), (), 0, REQUEST_COUNT)
    lengths = lengths.at[chosen].set(MAX_CACHED)
    emptied = (chosen + 1 + jax.random.randint(jax.random.fold_in(key, 24), (), 0, REQUEST_COUNT - 1)) % REQUEST_COUNT
    return lengths.at[emptied].set(0).astype(jnp.int32)


def draw_block_table(key, part):
    subkeys = jax.random.split(jax.random.fold_in(key, 31), REQUEST_COUNT)
    return jax.vmap(lambda subkey: jax.random.permutation(subkey, POOL_PAGES)[:PAGES])(subkeys).astype(jnp.int32)


def levels(key, dims, cuts, low, high):
    gain = 1.0
    for axis_at, parts in cuts:
        heights = jax.random.uniform(jax.random.fold_in(jax.random.fold_in(key, 6), axis_at), (parts,), jnp.float32, low / len(cuts), high / len(cuts))
        gain = gain * jnp.repeat(jnp.exp(heights), dims[axis_at] // parts).reshape((-1,) + (1,) * (len(dims) - 1 - axis_at))
    return gain


def scatter_about(stream_key, dims, scale, bound, shards=(), held_as=jnp.bfloat16):
    entries = jax.random.normal(stream_key, dims, jnp.float32) * scale
    if len(shards) > 0:
        entries = levels(stream_key, dims, shards, -0.22, 0.18) * entries
    return jnp.clip(entries, min=-bound, max=bound).astype(held_as)


def setup_inputs(seed: int = 0, part: int = 0) -> dict:
    key_of = jax.random.split(jax.random.key(seed), 9)
    part_keys = jax.random.split(jax.random.fold_in(key_of[8], part), 9)
    return {
        "queries": draw_queries(jax.random.fold_in(jax.random.fold_in(key_of[8], part), 71), part),
        "fresh_keys": draw_fresh_keys(jax.random.fold_in(jax.random.fold_in(key_of[8], part), 71), part),
        "fresh_values": scatter_about(part_keys[2], (ALL_TOKENS, KEY_VALUE_HEADS * HEAD_SIZE), 1.0, 4.0, ((0, 8), (1, 2))),
        "key_pool_pages": scatter_about(part_keys[3], (REQUEST_COUNT * POOL_PAGES, PAGE_TOKENS, KEY_VALUE_HEADS * HEAD_SIZE), 1.0, 4.0, ((0, 8), (2, 2))),
        "value_pool_pages": scatter_about(part_keys[4], (REQUEST_COUNT * POOL_PAGES, PAGE_TOKENS, KEY_VALUE_HEADS * HEAD_SIZE), 1.0, 4.0, ((0, 8), (2, 2))),
        "block_table": draw_block_table(jax.random.fold_in(jax.random.fold_in(key_of[8], part), 71), part),
        "prefix_lengths": draw_prefix_lengths(jax.random.fold_in(jax.random.fold_in(key_of[8], part), 71), part),
        "out_weight": scatter_about(key_of[7], (HQ * HEAD_SIZE, D), (HQ * HEAD_SIZE) ** -0.5, 0.09375, ((0, 2), (1, 8))),
    }


def reference(queries, fresh_keys, fresh_values, key_pool_pages, value_pool_pages, block_table, prefix_lengths, out_weight):
    score_scale = HEAD_SIZE ** -0.5

    def single(request_index):
        query_block = lax.dynamic_slice_in_dim(queries, request_index * REQUEST_TOKENS, REQUEST_TOKENS, 0).astype(jnp.float32).reshape(REQUEST_TOKENS, KEY_VALUE_HEADS, QUERY_GROUP, HEAD_SIZE)
        window_keys = lax.dynamic_slice_in_dim(fresh_keys, request_index * REQUEST_TOKENS, REQUEST_TOKENS, 0).reshape(REQUEST_TOKENS, KEY_VALUE_HEADS, HEAD_SIZE)
        window_values = lax.dynamic_slice_in_dim(fresh_values, request_index * REQUEST_TOKENS, REQUEST_TOKENS, 0).reshape(REQUEST_TOKENS, KEY_VALUE_HEADS, HEAD_SIZE)
        pool_page_block = lax.dynamic_slice_in_dim(key_pool_pages, request_index * POOL_PAGES, POOL_PAGES, 0)
        value_tile_block = lax.dynamic_slice_in_dim(value_pool_pages, request_index * POOL_PAGES, POOL_PAGES, 0)
        request_pages = block_table[request_index]
        stored_keys = jnp.take(pool_page_block, request_pages, axis=0).reshape(MAX_CACHED, KEY_VALUE_HEADS, HEAD_SIZE)
        stored_values = jnp.take(value_tile_block, request_pages, axis=0).reshape(MAX_CACHED, KEY_VALUE_HEADS, HEAD_SIZE)
        all_keys = jnp.concatenate([stored_keys, window_keys], 0).astype(jnp.float32)
        all_values = jnp.concatenate([stored_values, window_values], 0).astype(jnp.float32)
        key_index = jnp.arange(MAX_CACHED + REQUEST_TOKENS, dtype=jnp.int32)
        token_index = jnp.arange(REQUEST_TOKENS, dtype=jnp.int32)
        length = prefix_lengths[request_index]
        visible = jnp.where(key_index[None, :] < MAX_CACHED, key_index[None, :] < length,
                            (key_index[None, :] - MAX_CACHED) <= token_index[:, None])
        scores = jnp.einsum('tkgd,skd->kgts', query_block, all_keys) * score_scale
        scores = jnp.where(visible[None, None], scores, jnp.float32(-1e30))
        row_peak = scores.max(-1, keepdims=True)
        weights = jnp.where(visible[None, None], jnp.exp(scores - row_peak), jnp.float32(0.0))
        weight_sum = weights.sum(-1)
        rounded = lax.optimization_barrier(weights.astype(jnp.bfloat16)).astype(jnp.float32)
        weighted = jnp.einsum('kgts,skd->kgtd', rounded, all_values)
        attended = (weighted / weight_sum[..., None]).astype(jnp.bfloat16)
        return attended.transpose(2, 0, 1, 3).reshape(REQUEST_TOKENS, HQ * HEAD_SIZE)

    per_request = lax.map(single, jnp.arange(REQUEST_COUNT, dtype=jnp.int32))
    attended = per_request.reshape(ALL_TOKENS, HQ * HEAD_SIZE)
    return jnp.dot(attended, out_weight, preferred_element_type=jnp.float32).astype(jnp.bfloat16)
```

```python
import functools

import jax
import jax.numpy as jnp
from jax import lax
from jax.experimental import pallas as pl
from jax.experimental.pallas import tpu as pltpu
from jax.sharding import PartitionSpec as P

HEAD_SIZE = 128
QUERY_GROUP = 8
PAGE_TOKENS = 128
CHUNK = 256
OUTER_ZY = 7
INNER_ZY = 5
SCALE = HEAD_SIZE ** (-0.5) * 1.4426950408889634
MASKED = -1e30


def kernel(
    line, q_ref, fk_ref, fv_ref, kp_ref, vp_ref, table_ref, len_ref, w_ref, out_ref,
    wbuf, act, stage, keys, values, bias,
    w_recv, w_next, w_side, own_send, act_recv, act_send, act_fwd, out_send, out_recv,
):
    group, dp, core = lax.axis_index("groups"), lax.axis_index("dp"), lax.axis_index("tensor")
    z, y = dp // 2, dp % 2
    half = group % 2
    cousin = group + 1 - 2 * half
    other = 1 - core
    peer = z * 2 + 1 - y
    shards = line // 2
    part, cols = w_ref.shape
    tokens = q_ref.shape[0]
    per_core = part // CHUNK
    per_half = per_core // 2
    own_core = z // shards
    own_slot = z - own_core * shards
    wide = act.shape[2] // 2
    step_cols = wide // per_core
    heads_per_step = step_cols // HEAD_SIZE
    heads_per_kv = QUERY_GROUP
    tile = min(cols, 256)
    tiles = cols // tile

    def remote(src, dst, send, recv, where):
        return pltpu.make_async_remote_copy(
            src_ref=src, dst_ref=dst, send_sem=send, recv_sem=recv,
            device_id=where, device_id_type=pl.DeviceIdType.MESH,
        )

    def rows(k):
        return pl.ds(pl.multiple_of(k * CHUNK, CHUNK), CHUNK)

    barrier = pltpu.get_barrier_semaphore()

    def greet(where):
        pl.semaphore_signal(barrier, inc=1, device_id=where, device_id_type=pl.DeviceIdType.MESH)

    greet((group, dp, other))
    greet((cousin, dp, core))
    greet((group, peer, core))

    @pl.when(z > 0)
    def _():
        greet((group, dp - 2, core))
        greet((group, dp - 2, other))

    @pl.when(z < line - 1)
    def _():
        greet((group, dp + 2, core))
        greet((group, dp + 2, other))

    neighbours = jnp.where(z > 0, 2, 0) + jnp.where(z < line - 1, 2, 0)
    pl.semaphore_wait(barrier, 3 + neighbours)

    def own_copy(k, side):
        slab = core * per_core + k
        where = (group, dp + 2 * side, own_core) if side else (group, dp, other)
        return remote(
            w_ref.at[rows(k)], wbuf.at[own_slot, rows(slab)],
            own_send.at[side + 1, k], w_recv.at[own_slot, slab], where,
        )

    def own_local(k):
        slab = core * per_core + k
        return pltpu.make_async_copy(
            w_ref.at[rows(k)], wbuf.at[own_slot, rows(slab)], w_recv.at[own_slot, slab]
        )

    def each_own(act_on):
        def one(j, carry):
            k = half * per_half + j

            @pl.when(z > 0)
            def _():
                act_on(own_copy(k, -1))

            @pl.when(z < line - 1)
            def _():
                act_on(own_copy(k, 1))

            return carry

        lax.fori_loop(0, per_half, one, 0)

        @pl.when(core != own_core)
        def _():
            lax.fori_loop(0, per_core, lambda k, carry: (act_on(own_copy(k, 0)), carry)[1], 0)

    each_own(lambda copy: copy.start())

    @pl.when(core == own_core)
    def _():
        lax.fori_loop(0, per_core, lambda k, carry: (own_local(k).start(), carry)[1], 0)

    def slab_of(i, which):
        return (i % 2) * per_core + which * per_half + i // 2

    def landed(slot, slab):
        remote(
            wbuf.at[slot, rows(slab)], wbuf.at[slot, rows(slab)],
            w_next.at[slot, slab], w_recv.at[slot, slab], (group, dp, other),
        ).wait_recv()

    def next_copy(slot, slab, step):
        return remote(
            wbuf.at[slot, rows(slab)], wbuf.at[slot, rows(slab)],
            w_next.at[slot, slab], w_recv.at[slot, slab], (group, dp + 2 * step, core),
        )

    def side_copy(slot, slab):
        return remote(
            wbuf.at[slot, rows(slab)], wbuf.at[slot, rows(slab)],
            w_side.at[slot, slab], w_recv.at[slot, slab], (cousin, dp, core),
        )

    def pass_on(slot, origin, i):
        slab = slab_of(i, half)
        landed(slot, slab)

        @pl.when(jnp.logical_and(origin < z, z < line - 1))
        def _():
            next_copy(slot, slab, 1).start()

        @pl.when(jnp.logical_and(origin > z, z > 0))
        def _():
            next_copy(slot, slab, -1).start()

        side_copy(slot, slab).start()

    length = len_ref[dp]
    cached = table_ref.shape[1] * PAGE_TOKENS
    for j in range(table_ref.shape[1]):
        page = table_ref[0, j]
        keys[j * PAGE_TOKENS:(j + 1) * PAGE_TOKENS, :] = kp_ref[page]
        values[j * PAGE_TOKENS:(j + 1) * PAGE_TOKENS, :] = vp_ref[page]
    keys[cached:, :] = fk_ref[...]
    values[cached:, :] = fv_ref[...]
    position = lax.broadcasted_iota(jnp.int32, (tokens, cached), 1)
    bias[:, :cached] = jnp.where(position < length, 0.0, MASKED)
    bias[:, cached:] = jnp.where(
        lax.broadcasted_iota(jnp.int32, (tokens, tokens), 1)
        <= lax.broadcasted_iota(jnp.int32, (tokens, tokens), 0),
        0.0, MASKED,
    )

    def act_cols(slab):
        return pl.ds(pl.multiple_of(slab * step_cols, step_cols), step_cols)

    def act_copy(i, to_peer):
        slab = core * per_core + i
        src = act.at[0, :, act_cols(slab)]
        if to_peer:
            return remote(src, act.at[1, :, act_cols(slab)], act_send.at[1, i],
                          act_recv.at[1, slab], (group, peer, core))
        return remote(src, src, act_send.at[0, i], act_recv.at[0, slab], (group, dp, other))

    def act_forward(i):
        slab = core * per_core + i
        ref = act.at[1, :, act_cols(slab)]
        return remote(ref, ref, act_fwd.at[i], act_recv.at[1, slab], (group, dp, other))

    def act_landed(block, slab):
        ref = act.at[block, :, act_cols(slab)]
        remote(ref, ref, act_fwd.at[0], act_recv.at[block, slab], (group, dp, other)).wait_recv()

    def relay(i):
        act_landed(1, core * per_core + i)
        act_forward(i).start()

    lag = 2

    def attention_step(i, carry):
        kv = (i * heads_per_step) // heads_per_kv
        kv_cols = pl.ds(pl.multiple_of(kv * HEAD_SIZE, HEAD_SIZE), HEAD_SIZE)
        for n in range(heads_per_step):
            head = i * heads_per_step + n
            q = q_ref[:, pl.ds(pl.multiple_of(head * HEAD_SIZE, HEAD_SIZE), HEAD_SIZE)]
            scores = lax.dot_general(
                q, keys[:, kv_cols], (((1,), (1,)), ((), ())), preferred_element_type=jnp.float32
            )
            scores = scores * SCALE + bias[...]
            weights = jnp.exp2(scores - jnp.max(scores, axis=-1, keepdims=True))
            total = jnp.sum(weights, axis=-1, keepdims=True)
            weighted = jnp.dot(
                weights.astype(jnp.bfloat16), values[:, kv_cols], preferred_element_type=jnp.float32
            )
            start = core * wide + head * HEAD_SIZE
            act[0, :, pl.ds(pl.multiple_of(start, HEAD_SIZE), HEAD_SIZE)] = (
                weighted / total
            ).astype(jnp.bfloat16)
        act_copy(i, True).start()
        act_copy(i, False).start()
        for side in (-1, 1):
            origin = z + side

            @pl.when(jnp.logical_and(
                jnp.logical_and(origin >= core * shards, origin < (core + 1) * shards), True))
            def _():
                pass_on(origin - core * shards, origin, i)

        @pl.when(i >= lag)
        def _():
            relay(i - lag)

        return carry

    lax.fori_loop(0, per_core, attention_step, 0)
    for i in range(per_core - lag, per_core):
        relay(i)

    def origin_of(p):
        low = core * shards
        inside = low + (z - low + p + shards * line) % shards
        return jnp.where(z < low, low + p, jnp.where(z >= low + shards, low + shards - 1 - p, inside))

    def out_cols(origin, n):
        start = (origin * 2 + y - core * 2 * shards) * cols + n * tile
        return pl.ds(pl.multiple_of(start, 128), tile)

    def out_copy(slot, n, column):
        return remote(
            stage.at[slot, n], out_ref.at[:, column], out_send.at[slot, n],
            out_recv.at[slot, n], (group, peer, core),
        )

    def product(block, slot, n):
        return jnp.dot(
            act[block], wbuf[slot, :, pl.ds(pl.multiple_of(n * tile, 128), tile)],
            preferred_element_type=jnp.float32,
        ).astype(jnp.bfloat16)

    def piece(origin, m):
        slot = origin - core * shards
        n = m % tiles
        column = out_cols(origin, n)

        @pl.when(m < tiles)
        def _():
            stage[slot, n] = product(1, slot, n)
            out_copy(slot, n, column).start()

        @pl.when(m >= tiles)
        def _():
            out_ref[:, column] = product(0, slot, n)

    def rest_landed(origin):
        slot = origin - core * shards

        def one(i, carry):
            landed(slot, slab_of(i, 1 - half))

            @pl.when(origin == z)
            def _():
                landed(slot, slab_of(i, half))

            return carry

        lax.fori_loop(0, per_core, one, 0)

    def acts_landed():
        def one(i, carry):
            act_landed(0, other * per_core + i)
            act_landed(1, other * per_core + i)
            return carry

        lax.fori_loop(0, per_core, one, 0)

    def shard_step(p, carry):
        origin = origin_of(p)
        before = origin_of(jnp.maximum(p - 1, 0))

        def chunk_step(i, inner):
            @pl.when(jnp.logical_or(origin > z + 1, origin < z - 1))
            def _():
                pass_on(origin - core * shards, origin, i)

            return inner

        lax.fori_loop(0, per_core, chunk_step, 0)

        @pl.when(p > 0)
        def _():
            @pl.when(p == 1)
            def _():
                acts_landed()

            rest_landed(before)
            lax.fori_loop(0, 2 * tiles, lambda m, inner: (piece(before, m), inner)[1], 0)

        return carry

    lax.fori_loop(0, shards, shard_step, 0)
    if shards == 1:
        acts_landed()
    last = origin_of(shards - 1)
    rest_landed(last)
    lax.fori_loop(0, 2 * tiles, lambda m, carry: (piece(last, m), carry)[1], 0)

    def finish(slot, carry):
        origin = core * shards + slot
        for n in range(tiles):
            start = (origin * 2 + 1 - y - core * 2 * shards) * cols + n * tile
            copy = out_copy(slot, n, pl.ds(pl.multiple_of(start, 128), tile))
            copy.wait_recv()
            copy.wait_send()

        @pl.when(origin != z)
        def _():
            def one(i, inner):
                slab = slab_of(i, half)

                @pl.when(jnp.logical_and(origin < z, z < line - 1))
                def _():
                    next_copy(slot, slab, 1).wait_send()

                @pl.when(jnp.logical_and(origin > z, z > 0))
                def _():
                    next_copy(slot, slab, -1).wait_send()

                side_copy(slot, slab).wait_send()
                return inner

            lax.fori_loop(0, per_core, one, 0)

        return carry

    lax.fori_loop(0, shards, finish, 0)

    def acts_sent(i, carry):
        act_copy(i, True).wait_send()
        act_copy(i, False).wait_send()
        act_forward(i).wait_send()
        return carry

    lax.fori_loop(0, per_core, acts_sent, 0)
    each_own(lambda copy: copy.wait_send())


def shards_program(line, queries, fresh_keys, fresh_values, key_pages, value_pages, table, lengths, weight):
    tokens, wide = queries.shape
    part, cols = weight.shape
    per_core = part // CHUNK
    shards = line // 2
    tile = min(cols, 256)
    tiles = cols // tile
    span = table.shape[1] * PAGE_TOKENS + tokens
    kv_width = fresh_keys.shape[1]
    out_width = 2 * shards * cols
    vmem = pl.BlockSpec(memory_space=pltpu.VMEM)
    smem = pl.BlockSpec(memory_space=pltpu.SMEM)
    dma = pltpu.SemaphoreType.DMA
    heads = wide // HEAD_SIZE
    flops = 4 * heads * tokens * span * HEAD_SIZE + 2 * 2 * tokens * 2 * part * shards * cols
    return pl.pallas_call(
        functools.partial(kernel, line),
        out_shape=jax.ShapeDtypeStruct((tokens, out_width), jnp.bfloat16),
        in_specs=[vmem, vmem, vmem, vmem, vmem, smem, smem, pl.BlockSpec(memory_space=pl.ANY)],
        out_specs=vmem,
        scratch_shapes=[
            pltpu.VMEM((shards, 2 * part, cols), jnp.bfloat16),
            pltpu.VMEM((2, tokens, 2 * wide), jnp.bfloat16),
            pltpu.VMEM((shards, tiles, tokens, tile), jnp.bfloat16),
            pltpu.VMEM((span, kv_width), jnp.bfloat16),
            pltpu.VMEM((span, kv_width), jnp.bfloat16),
            pltpu.VMEM((tokens, span), jnp.float32),
            dma((shards, 2 * per_core)),
            dma((shards, 2 * per_core)),
            dma((shards, 2 * per_core)),
            dma((3, per_core)),
            dma((2, 2 * per_core)),
            dma((2, per_core)),
            dma((per_core,)),
            dma((shards, tiles)),
            dma((shards, tiles)),
        ],
        compiler_params=pltpu.CompilerParams(
            collective_id=0, has_side_effects=True, vmem_limit_bytes=60 * 1024 * 1024
        ),
        cost_estimate=pl.CostEstimate(
            flops=flops, bytes_accessed=8 * 1024 * 1024, transcendentals=heads * tokens * span
        ),
    )(queries, fresh_keys, fresh_values, key_pages, value_pages, table, lengths, weight)


def square_kernel(
    line, q_ref, fk_ref, fv_ref, kp_ref, vp_ref, table_ref, len_ref, w_ref, out_ref,
    act, wall, relay, px_out, px_in, keep, stage, keys, values, bias,
    w_recv, w_send, w_side, r_recv, own_sem, act_recv, act_send, act_fwd,
    px_recv, px_send, out_recv, out_send,
):
    group, dp, core = lax.axis_index("groups"), lax.axis_index("dp"), lax.axis_index("tensor")
    z, y = dp // 2, dp % 2
    x = group % 2
    cousin = group + 1 - 2 * x
    other = 1 - core
    half = z // 2
    inner = z % 2 != half
    outer = jnp.logical_not(inner)
    zp = z + 1 - 2 * (z % 2)
    zm = jnp.where(inner, line - 1 - z, z)
    peer = z * 2 + 1 - y
    part, cols = w_ref.shape
    tokens, wide = q_ref.shape
    chunks = part // CHUNK
    unit = cols // 2
    rows_mine = tokens // 2
    steps = wide // 256
    step_cols = wide // steps
    heads_per_step = step_cols // HEAD_SIZE
    near, far = steps * OUTER_ZY // 8, steps * INNER_ZY // 8
    first = min(2, chunks)

    def remote(src, dst, send, recv, where):
        return pltpu.make_async_remote_copy(
            src_ref=src, dst_ref=dst, send_sem=send, recv_sem=recv,
            device_id=where, device_id_type=pl.DeviceIdType.MESH,
        )

    def loop(low, high, act_on):
        lax.fori_loop(low, high, lambda k, carry: (act_on(k), carry)[1], 0)

    def rows(k):
        return pl.ds(pl.multiple_of(k * CHUNK, CHUNK), CHUNK)

    barrier = pltpu.get_barrier_semaphore()

    def greet(where):
        pl.semaphore_signal(barrier, inc=1, device_id=where, device_id_type=pl.DeviceIdType.MESH)

    greet((group, dp, other))
    for chip in (peer, zp * 2 + y, zp * 2 + 1 - y):
        greet((group, chip, core))
        greet((group, chip, other))

    @pl.when(inner)
    def _():
        greet((cousin, dp, core))
        greet((group, zm * 2 + y, core))

    pl.semaphore_wait(barrier, 7 + jnp.where(inner, 2, 0))

    half_cols = pl.ds(pl.multiple_of(x * unit, 128), unit)

    def mid_own(k):
        return remote(
            w_ref.at[rows(k), half_cols], wall.at[1, x, rows(k)],
            w_send.at[0, k], w_recv.at[0, x, k], (group, zm * 2 + y, core),
        )

    def to_relay(k):
        return remote(
            w_ref.at[rows(k), half_cols], relay.at[rows(k)],
            w_send.at[0, k], r_recv.at[k], (group, zp * 2 + y, core),
        )

    def mid_relay(k):
        return remote(
            relay.at[rows(k)], wall.at[2, x, rows(k)],
            w_send.at[1, k], w_recv.at[1, x, k], (group, zm * 2 + y, core),
        )

    def side(s, k):
        ref = wall.at[s, x, rows(k)]
        return remote(ref, ref, w_side.at[s - 1, k], w_recv.at[s - 1, x, k], (cousin, dp, core))

    def w_landed(s, u, k):
        ref = wall.at[s, u, rows(k)]
        remote(ref, ref, w_side.at[s - 1, k], w_recv.at[s - 1, u, k], (cousin, dp, core)).wait_recv()

    def relay_on(k):
        to_relay(k).wait_recv()
        mid_relay(k).start()

    def side_on(s, k):
        w_landed(s, x, k)
        side(s, k).start()

    def own_copy(u):
        return pltpu.make_async_copy(
            w_ref.at[:, u * unit:(u + 1) * unit], wall.at[0, u], own_sem.at[u]
        )

    @pl.when(inner)
    def _():
        loop(0, chunks, lambda k: mid_own(k).start())

    @pl.when(outer)
    def _():
        loop(0, first, lambda k: to_relay(k).start())

    own_copy(0).start()
    own_copy(1).start()

    length = len_ref[dp]
    cached = table_ref.shape[1] * PAGE_TOKENS
    for j in range(table_ref.shape[1]):
        page = table_ref[0, j]
        keys[j * PAGE_TOKENS:(j + 1) * PAGE_TOKENS, :] = kp_ref[page]
        values[j * PAGE_TOKENS:(j + 1) * PAGE_TOKENS, :] = vp_ref[page]
    keys[cached:, :] = fk_ref[...]
    values[cached:, :] = fv_ref[...]
    position = lax.broadcasted_iota(jnp.int32, (tokens, cached), 1)
    bias[:, :cached] = jnp.where(position < length, 0.0, MASKED)
    bias[:, cached:] = jnp.where(
        lax.broadcasted_iota(jnp.int32, (tokens, tokens), 1)
        <= lax.broadcasted_iota(jnp.int32, (tokens, tokens), 0),
        0.0, MASKED,
    )

    def act_at(slot, i):
        return act.at[slot, :, pl.ds(pl.multiple_of(i * step_cols, step_cols), step_cols)]

    def act_y(i):
        return remote(act_at(0, i), act_at(1, i), act_send.at[0, i], act_recv.at[0, i],
                      (group, peer, core))

    def act_z(i):
        return remote(act_at(0, i), act_at(2, i), act_send.at[1, i], act_recv.at[1, i],
                      (group, zp * 2 + y, core))

    def on_y(i):
        return remote(act_at(2, i), act_at(3, i), act_fwd.at[0, i], act_recv.at[2, i],
                      (group, peer, core))

    def on_z(i):
        return remote(act_at(1, i), act_at(3, i), act_fwd.at[1, i], act_recv.at[2, i],
                      (group, zp * 2 + y, core))

    over_y = jnp.where(inner, near, far)
    over_z = jnp.where(inner, far, near)

    def act_on(i):
        act_y(i).wait_recv()

        @pl.when(i >= over_z)
        def _():
            on_z(i).start()

        act_z(i).wait_recv()

        @pl.when(i < over_y)
        def _():
            on_y(i).start()

    lag = 2

    def attention_step(i):
        kv = (i * heads_per_step) // QUERY_GROUP
        kv_cols = pl.ds(pl.multiple_of(kv * HEAD_SIZE, HEAD_SIZE), HEAD_SIZE)
        for n in range(heads_per_step):
            start = pl.multiple_of((i * heads_per_step + n) * HEAD_SIZE, HEAD_SIZE)
            q = q_ref[:, pl.ds(start, HEAD_SIZE)]
            scores = lax.dot_general(
                q, keys[:, kv_cols], (((1,), (1,)), ((), ())), preferred_element_type=jnp.float32
            )
            scores = scores * SCALE + bias[...]
            weights = jnp.exp2(scores - jnp.max(scores, axis=-1, keepdims=True))
            total = jnp.sum(weights, axis=-1, keepdims=True)
            weighted = jnp.dot(
                weights.astype(jnp.bfloat16), values[:, kv_cols], preferred_element_type=jnp.float32
            )
            act[0, :, pl.ds(start, HEAD_SIZE)] = (weighted / total).astype(jnp.bfloat16)
        act_y(i).start()
        act_z(i).start()

        @pl.when(i >= lag)
        def _():
            act_on(i - lag)

            @pl.when(inner)
            def _():
                side_on(1, i - lag)

    loop(0, steps, attention_step)

    @pl.when(outer)
    def _():
        loop(first, chunks, lambda k: to_relay(k).start())

    def shard_z(s):
        return jnp.where(s == 0, z, jnp.where(s == 1, zm, (line - 1) * (1 - half)))

    def task(s, u, slot):
        return (s * 2 + u) * 4 + slot

    def swap(t):
        return remote(px_out.at[t], px_in.at[t], px_send.at[t], px_recv.at[t], (group, dp, other))

    def place(s, u):
        zs = shard_z(s)
        to = zs // 2
        column = (zs * 2 + y - to * line) * cols + u * unit
        spot = ((zs % 2) * 2 + y) * 4 + u * 2 + core
        ref = out_ref.at[pl.ds(pl.multiple_of(core * rows_mine, rows_mine), rows_mine),
                         pl.ds(pl.multiple_of(column, 128), unit)]
        return to, ref, spot

    def out_copy(s, u, slot):
        to, ref, spot = place(s, u)
        t = task(s, u, slot)
        zd = jnp.where(slot >= 2, zp, z)
        yd = jnp.where(slot % 2 == 1, 1 - y, y)
        return remote(stage.at[t], ref, out_send.at[t], out_recv.at[spot], (group, zd * 2 + yd, to))

    def stays(s, slot):
        return jnp.logical_and(slot == 0, shard_z(s) // 2 == core)

    def begin(s, u, slot):
        t = task(s, u, slot)
        keep[t] = jnp.dot(act[slot], wall[s, u], preferred_element_type=jnp.float32)
        start = pl.multiple_of(other * rows_mine, rows_mine)
        px_out[t] = keep[t, pl.ds(start, rows_mine), :].astype(jnp.bfloat16)
        swap(t).start()

    def finish(s, u, slot):
        t = task(s, u, slot)
        swap(t).wait_recv()
        start = pl.multiple_of(core * rows_mine, rows_mine)
        stage[t] = (keep[t, pl.ds(start, rows_mine), :] + px_in[t].astype(jnp.float32)).astype(jnp.bfloat16)

        @pl.when(stays(s, slot))
        def _():
            to, ref, spot = place(s, u)
            pltpu.make_async_copy(stage.at[t], ref, out_recv.at[spot]).start()

        @pl.when(jnp.logical_not(stays(s, slot)))
        def _():
            out_copy(s, u, slot).start()

    def run(low, high, which):
        def one(n):
            begin(*which(n))

            @pl.when(n > low)
            def _():
                finish(*which(n - 1))

        loop(low, high, one)

    loop(steps - lag, steps, act_on)
    own_copy(0).wait()
    own_copy(1).wait()

    def corner_landed():
        loop(0, steps, lambda i: on_y(i).wait_recv())

    @pl.when(outer)
    def _():
        def which(n):
            return 0, n % 2, n // 2

        run(0, 6, which)
        corner_landed()
        finish(*which(5))
        run(6, 8, which)
        finish(*which(7))

    @pl.when(inner)
    def _():
        loop(steps - lag, chunks, lambda k: side_on(1, k))
        loop(0, first, relay_on)
        loop(0, chunks, lambda k: w_landed(1, 1 - x, k))

        def which(n):
            return (n % 4) // 2, n % 2, n // 4

        per = 12 // (chunks - first)

        def mixed(k):
            relay_on(k)
            for m in range(per):
                n = (k - first) * per + m
                begin(*which(n))

                @pl.when(n > 0)
                def _():
                    finish(*which(n - 1))

            side_on(2, k - first)

        loop(first, chunks, mixed)
        run(per * (chunks - first), 12, which)
        finish(*which(11))
        loop(chunks - first, chunks - 1, lambda k: side_on(2, k))
        corner_landed()
        run(12, 16, which)
        finish(*which(15))
        side_on(2, chunks - 1)

        def last(n):
            return 2, jnp.where(n < 4, x, 1 - x), n % 4

        run(0, 4, last)
        loop(0, chunks, lambda k: w_landed(2, 1 - x, k))
        finish(*last(3))
        run(4, 8, last)
        finish(*last(7))

    def drain(t):
        swap(t).wait_send()
        s, u, slot = t // 8, (t // 4) % 2, t % 4

        @pl.when(jnp.logical_not(stays(s, slot)))
        def _():
            out_copy(s, u, slot).wait_send()

    loop(0, jnp.where(inner, 24, 8), drain)

    def act_sent(i):
        act_y(i).wait_send()
        act_z(i).wait_send()

        @pl.when(i >= over_z)
        def _():
            on_z(i).wait_send()

        @pl.when(i < over_y)
        def _():
            on_y(i).wait_send()

    loop(0, steps, act_sent)

    def weight_sent(k):
        @pl.when(outer)
        def _():
            to_relay(k).wait_send()

        @pl.when(inner)
        def _():
            mid_own(k).wait_send()
            mid_relay(k).wait_send()
            side(1, k).wait_send()
            side(2, k).wait_send()

    loop(0, chunks, weight_sent)

    def out_landed(n):
        column = pl.ds(pl.multiple_of((n // 2) * unit, 128), unit)
        ref = out_ref.at[pl.ds(pl.multiple_of((n % 2) * rows_mine, rows_mine), rows_mine), column]
        remote(stage.at[0], ref, out_send.at[0], out_recv.at[n], (group, dp, other)).wait_recv()

    loop(0, 16, out_landed)


def square_program(line, queries, fresh_keys, fresh_values, key_pages, value_pages, table, lengths, weight):
    tokens, wide = queries.shape
    part, cols = weight.shape
    chunks = part // CHUNK
    steps = wide // 256
    unit = cols // 2
    span = table.shape[1] * PAGE_TOKENS + tokens
    kv_width = fresh_keys.shape[1]
    vmem = pl.BlockSpec(memory_space=pltpu.VMEM)
    smem = pl.BlockSpec(memory_space=pltpu.SMEM)
    dma = pltpu.SemaphoreType.DMA
    bf16, f32 = jnp.bfloat16, jnp.float32
    heads = wide // HEAD_SIZE
    flops = 4 * heads * tokens * span * HEAD_SIZE + 2 * 24 * tokens * part * unit
    return pl.pallas_call(
        functools.partial(square_kernel, line),
        out_shape=jax.ShapeDtypeStruct((tokens, line * cols), bf16),
        in_specs=[vmem, vmem, vmem, vmem, vmem, smem, smem, pl.BlockSpec(memory_space=pl.ANY)],
        out_specs=vmem,
        scratch_shapes=[
            pltpu.VMEM((4, tokens, wide), bf16),
            pltpu.VMEM((3, 2, part, unit), bf16),
            pltpu.VMEM((part, unit), bf16),
            pltpu.VMEM((24, tokens // 2, unit), bf16),
            pltpu.VMEM((24, tokens // 2, unit), bf16),
            pltpu.VMEM((24, tokens, unit), f32),
            pltpu.VMEM((24, tokens // 2, unit), bf16),
            pltpu.VMEM((span, kv_width), bf16),
            pltpu.VMEM((span, kv_width), bf16),
            pltpu.VMEM((tokens, span), f32),
            dma((2, 2, chunks)),
            dma((2, chunks)),
            dma((2, chunks)),
            dma((chunks,)),
            dma((2,)),
            dma((3, steps)),
            dma((2, steps)),
            dma((2, steps)),
            dma((24,)),
            dma((24,)),
            dma((16,)),
            dma((24,)),
        ],
        compiler_params=pltpu.CompilerParams(
            collective_id=0, has_side_effects=True, vmem_limit_bytes=60 * 1024 * 1024
        ),
        cost_estimate=pl.CostEstimate(
            flops=flops, bytes_accessed=8 * 1024 * 1024, transcendentals=heads * tokens * span
        ),
    )(queries, fresh_keys, fresh_values, key_pages, value_pages, table, lengths, weight)


def program_of(line):
    return square_program if line == 4 else shards_program


def solution(mesh):
    return jax.shard_map(
        functools.partial(program_of(mesh.shape["dp"] // 2), mesh.shape["dp"] // 2),
        mesh=mesh,
        in_specs=(
            P(("groups", "dp"), "tensor"),
            P(("groups", "dp"), "tensor"),
            P(("groups", "dp"), "tensor"),
            P(("groups", "dp"), None, "tensor"),
            P(("groups", "dp"), None, "tensor"),
            P(("groups", "dp"), None),
            P("groups"),
            P("tensor", "dp"),
        ),
        out_specs=P(("groups", "dp"), "tensor"),
        check_vma=False,
    )
```

```python
import functools

import jax
import jax.numpy as jnp
from jax import lax
from jax.experimental import pallas as pl
from jax.experimental.pallas import tpu as pltpu
from jax.sharding import PartitionSpec as P

HEAD_SIZE = 128
QUERY_GROUP = 8
PAGE_TOKENS = 128
CHUNK = 256
OUTER_ZY = 7
INNER_ZY = 5
SCALE = HEAD_SIZE ** (-0.5) * 1.4426950408889634
MASKED = -1e30


def kernel(
    line, q_ref, fk_ref, fv_ref, kp_ref, vp_ref, table_ref, len_ref, w_ref, out_ref,
    wbuf, act, stage, keys, values, bias,
    w_recv, w_next, w_side, own_send, act_recv, act_send, act_fwd, out_send, out_recv,
):
    group, dp, core = lax.axis_index("groups"), lax.axis_index("dp"), lax.axis_index("tensor")
    z, y = dp // 2, dp % 2
    half = group % 2
    cousin = group + 1 - 2 * half
    other = 1 - core
    peer = z * 2 + 1 - y
    shards = line // 2
    part, cols = w_ref.shape
    tokens = q_ref.shape[0]
    per_core = part // CHUNK
    per_half = per_core // 2
    own_core = z // shards
    own_slot = z - own_core * shards
    wide = act.shape[2] // 2
    step_cols = wide // per_core
    heads_per_step = step_cols // HEAD_SIZE
    heads_per_kv = QUERY_GROUP
    tile = min(cols, 256)
    tiles = cols // tile

    def remote(src, dst, send, recv, where):
        return pltpu.make_async_remote_copy(
            src_ref=src, dst_ref=dst, send_sem=send, recv_sem=recv,
            device_id=where, device_id_type=pl.DeviceIdType.MESH,
        )

    def rows(k):
        return pl.ds(pl.multiple_of(k * CHUNK, CHUNK), CHUNK)

    barrier = pltpu.get_barrier_semaphore()

    def greet(where):
        pl.semaphore_signal(barrier, inc=1, device_id=where, device_id_type=pl.DeviceIdType.MESH)

    greet((group, dp, other))
    greet((cousin, dp, core))
    greet((group, peer, core))

    @pl.when(z > 0)
    def _():
        greet((group, dp - 2, core))
        greet((group, dp - 2, other))

    @pl.when(z < line - 1)
    def _():
        greet((group, dp + 2, core))
        greet((group, dp + 2, other))

    neighbours = jnp.where(z > 0, 2, 0) + jnp.where(z < line - 1, 2, 0)
    pl.semaphore_wait(barrier, 3 + neighbours)

    def own_copy(k, side):
        slab = core * per_core + k
        where = (group, dp + 2 * side, own_core) if side else (group, dp, other)
        return remote(
            w_ref.at[rows(k)], wbuf.at[own_slot, rows(slab)],
            own_send.at[side + 1, k], w_recv.at[own_slot, slab], where,
        )

    def own_local(k):
        slab = core * per_core + k
        return pltpu.make_async_copy(
            w_ref.at[rows(k)], wbuf.at[own_slot, rows(slab)], w_recv.at[own_slot, slab]
        )

    def each_own(act_on):
        def one(j, carry):
            k = half * per_half + j

            @pl.when(z > 0)
            def _():
                act_on(own_copy(k, -1))

            @pl.when(z < line - 1)
            def _():
                act_on(own_copy(k, 1))

            return carry

        lax.fori_loop(0, per_half, one, 0)

        @pl.when(core != own_core)
        def _():
            lax.fori_loop(0, per_core, lambda k, carry: (act_on(own_copy(k, 0)), carry)[1], 0)

    each_own(lambda copy: copy.start())

    @pl.when(core == own_core)
    def _():
        lax.fori_loop(0, per_core, lambda k, carry: (own_local(k).start(), carry)[1], 0)

    def slab_of(i, which):
        return (i % 2) * per_core + which * per_half + i // 2

    def landed(slot, slab):
        remote(
            wbuf.at[slot, rows(slab)], wbuf.at[slot, rows(slab)],
            w_next.at[slot, slab], w_recv.at[slot, slab], (group, dp, other),
        ).wait_recv()

    def next_copy(slot, slab, step):
        return remote(
            wbuf.at[slot, rows(slab)], wbuf.at[slot, rows(slab)],
            w_next.at[slot, slab], w_recv.at[slot, slab], (group, dp + 2 * step, core),
        )

    def side_copy(slot, slab):
        return remote(
            wbuf.at[slot, rows(slab)], wbuf.at[slot, rows(slab)],
            w_side.at[slot, slab], w_recv.at[slot, slab], (cousin, dp, core),
        )

    def pass_on(slot, origin, i):
        slab = slab_of(i, half)
        landed(slot, slab)

        @pl.when(jnp.logical_and(origin < z, z < line - 1))
        def _():
            next_copy(slot, slab, 1).start()

        @pl.when(jnp.logical_and(origin > z, z > 0))
        def _():
            next_copy(slot, slab, -1).start()

        side_copy(slot, slab).start()

    length = len_ref[dp]
    cached = table_ref.shape[1] * PAGE_TOKENS
    for j in range(table_ref.shape[1]):
        page = table_ref[0, j]
        keys[j * PAGE_TOKENS:(j + 1) * PAGE_TOKENS, :] = kp_ref[page]
        values[j * PAGE_TOKENS:(j + 1) * PAGE_TOKENS, :] = vp_ref[page]
    keys[cached:, :] = fk_ref[...]
    values[cached:, :] = fv_ref[...]
    position = lax.broadcasted_iota(jnp.int32, (tokens, cached), 1)
    bias[:, :cached] = jnp.where(position < length, 0.0, MASKED)
    bias[:, cached:] = jnp.where(
        lax.broadcasted_iota(jnp.int32, (tokens, tokens), 1)
        <= lax.broadcasted_iota(jnp.int32, (tokens, tokens), 0),
        0.0, MASKED,
    )

    def act_cols(slab):
        return pl.ds(pl.multiple_of(slab * step_cols, step_cols), step_cols)

    def act_copy(i, to_peer):
        slab = core * per_core + i
        src = act.at[0, :, act_cols(slab)]
        if to_peer:
            return remote(src, act.at[1, :, act_cols(slab)], act_send.at[1, i],
                          act_recv.at[1, slab], (group, peer, core))
        return remote(src, src, act_send.at[0, i], act_recv.at[0, slab], (group, dp, other))

    def act_forward(i):
        slab = core * per_core + i
        ref = act.at[1, :, act_cols(slab)]
        return remote(ref, ref, act_fwd.at[i], act_recv.at[1, slab], (group, dp, other))

    def act_landed(block, slab):
        ref = act.at[block, :, act_cols(slab)]
        remote(ref, ref, act_fwd.at[0], act_recv.at[block, slab], (group, dp, other)).wait_recv()

    def relay(i):
        act_landed(1, core * per_core + i)
        act_forward(i).start()

    lag = 2

    def attention_step(i, carry):
        kv = (i * heads_per_step) // heads_per_kv
        kv_cols = pl.ds(pl.multiple_of(kv * HEAD_SIZE, HEAD_SIZE), HEAD_SIZE)
        for n in range(heads_per_step):
            head = i * heads_per_step + n
            q = q_ref[:, pl.ds(pl.multiple_of(head * HEAD_SIZE, HEAD_SIZE), HEAD_SIZE)]
            scores = lax.dot_general(
                q, keys[:, kv_cols], (((1,), (1,)), ((), ())), preferred_element_type=jnp.float32
            )
            scores = scores * SCALE + bias[...]
            weights = jnp.exp2(scores - jnp.max(scores, axis=-1, keepdims=True))
            total = jnp.sum(weights, axis=-1, keepdims=True)
            weighted = jnp.dot(
                weights.astype(jnp.bfloat16), values[:, kv_cols], preferred_element_type=jnp.float32
            )
            start = core * wide + head * HEAD_SIZE
            act[0, :, pl.ds(pl.multiple_of(start, HEAD_SIZE), HEAD_SIZE)] = (
                weighted / total
            ).astype(jnp.bfloat16)
        act_copy(i, True).start()
        act_copy(i, False).start()
        for side in (-1, 1):
            origin = z + side

            @pl.when(jnp.logical_and(
                jnp.logical_and(origin >= core * shards, origin < (core + 1) * shards), True))
            def _():
                pass_on(origin - core * shards, origin, i)

        @pl.when(i >= lag)
        def _():
            relay(i - lag)

        return carry

    lax.fori_loop(0, per_core, attention_step, 0)
    for i in range(per_core - lag, per_core):
        relay(i)

    def origin_of(p):
        low = core * shards
        inside = low + (z - low + p + shards * line) % shards
        return jnp.where(z < low, low + p, jnp.where(z >= low + shards, low + shards - 1 - p, inside))

    def out_cols(origin, n):
        start = (origin * 2 + y - core * 2 * shards) * cols + n * tile
        return pl.ds(pl.multiple_of(start, 128), tile)

    def out_copy(slot, n, column):
        return remote(
            stage.at[slot, n], out_ref.at[:, column], out_send.at[slot, n],
            out_recv.at[slot, n], (group, peer, core),
        )

    def product(block, slot, n):
        return jnp.dot(
            act[block], wbuf[slot, :, pl.ds(pl.multiple_of(n * tile, 128), tile)],
            preferred_element_type=jnp.float32,
        ).astype(jnp.bfloat16)

    def piece(origin, m):
        slot = origin - core * shards
        n = m % tiles
        column = out_cols(origin, n)

        @pl.when(m < tiles)
        def _():
            stage[slot, n] = product(1, slot, n)
            out_copy(slot, n, column).start()

        @pl.when(m >= tiles)
        def _():
            out_ref[:, column] = product(0, slot, n)

    def rest_landed(origin):
        slot = origin - core * shards

        def one(i, carry):
            landed(slot, slab_of(i, 1 - half))

            @pl.when(origin == z)
            def _():
                landed(slot, slab_of(i, half))

            return carry

        lax.fori_loop(0, per_core, one, 0)

    def acts_landed():
        def one(i, carry):
            act_landed(0, other * per_core + i)
            act_landed(1, other * per_core + i)
            return carry

        lax.fori_loop(0, per_core, one, 0)

    def shard_step(p, carry):
        origin = origin_of(p)
        before = origin_of(jnp.maximum(p - 1, 0))

        def chunk_step(i, inner):
            @pl.when(jnp.logical_or(origin > z + 1, origin < z - 1))
            def _():
                pass_on(origin - core * shards, origin, i)

            return inner

        lax.fori_loop(0, per_core, chunk_step, 0)

        @pl.when(p > 0)
        def _():
            @pl.when(p == 1)
            def _():
                acts_landed()

            rest_landed(before)
            lax.fori_loop(0, 2 * tiles, lambda m, inner: (piece(before, m), inner)[1], 0)

        return carry

    lax.fori_loop(0, shards, shard_step, 0)
    if shards == 1:
        acts_landed()
    last = origin_of(shards - 1)
    rest_landed(last)
    lax.fori_loop(0, 2 * tiles, lambda m, carry: (piece(last, m), carry)[1], 0)

    def finish(slot, carry):
        origin = core * shards + slot
        for n in range(tiles):
            start = (origin * 2 + 1 - y - core * 2 * shards) * cols + n * tile
            copy = out_copy(slot, n, pl.ds(pl.multiple_of(start, 128), tile))
            copy.wait_recv()
            copy.wait_send()

        @pl.when(origin != z)
        def _():
            def one(i, inner):
                slab = slab_of(i, half)

                @pl.when(jnp.logical_and(origin < z, z < line - 1))
                def _():
                    next_copy(slot, slab, 1).wait_send()

                @pl.when(jnp.logical_and(origin > z, z > 0))
                def _():
                    next_copy(slot, slab, -1).wait_send()

                side_copy(slot, slab).wait_send()
                return inner

            lax.fori_loop(0, per_core, one, 0)

        return carry

    lax.fori_loop(0, shards, finish, 0)

    def acts_sent(i, carry):
        act_copy(i, True).wait_send()
        act_copy(i, False).wait_send()
        act_forward(i).wait_send()
        return carry

    lax.fori_loop(0, per_core, acts_sent, 0)
    each_own(lambda copy: copy.wait_send())


def shards_program(line, queries, fresh_keys, fresh_values, key_pages, value_pages, table, lengths, weight):
    tokens, wide = queries.shape
    part, cols = weight.shape
    per_core = part // CHUNK
    shards = line // 2
    tile = min(cols, 256)
    tiles = cols // tile
    span = table.shape[1] * PAGE_TOKENS + tokens
    kv_width = fresh_keys.shape[1]
    out_width = 2 * shards * cols
    vmem = pl.BlockSpec(memory_space=pltpu.VMEM)
    smem = pl.BlockSpec(memory_space=pltpu.SMEM)
    dma = pltpu.SemaphoreType.DMA
    heads = wide // HEAD_SIZE
    flops = 4 * heads * tokens * span * HEAD_SIZE + 2 * 2 * tokens * 2 * part * shards * cols
    return pl.pallas_call(
        functools.partial(kernel, line),
        out_shape=jax.ShapeDtypeStruct((tokens, out_width), jnp.bfloat16),
        in_specs=[vmem, vmem, vmem, vmem, vmem, smem, smem, pl.BlockSpec(memory_space=pl.ANY)],
        out_specs=vmem,
        scratch_shapes=[
            pltpu.VMEM((shards, 2 * part, cols), jnp.bfloat16),
            pltpu.VMEM((2, tokens, 2 * wide), jnp.bfloat16),
            pltpu.VMEM((shards, tiles, tokens, tile), jnp.bfloat16),
            pltpu.VMEM((span, kv_width), jnp.bfloat16),
            pltpu.VMEM((span, kv_width), jnp.bfloat16),
            pltpu.VMEM((tokens, span), jnp.float32),
            dma((shards, 2 * per_core)),
            dma((shards, 2 * per_core)),
            dma((shards, 2 * per_core)),
            dma((3, per_core)),
            dma((2, 2 * per_core)),
            dma((2, per_core)),
            dma((per_core,)),
            dma((shards, tiles)),
            dma((shards, tiles)),
        ],
        compiler_params=pltpu.CompilerParams(
            collective_id=0, has_side_effects=True, vmem_limit_bytes=60 * 1024 * 1024
        ),
        cost_estimate=pl.CostEstimate(
            flops=flops, bytes_accessed=8 * 1024 * 1024, transcendentals=heads * tokens * span
        ),
    )(queries, fresh_keys, fresh_values, key_pages, value_pages, table, lengths, weight)


def square_kernel(
    line, q_hbm, fk_hbm, fv_hbm, kp_hbm, vp_hbm, table_ref, len_ref, w_ref, out_ref,
    q_ref, kp_ref, vp_ref, act, wall, relay, px_out, px_in, keep, stage, keys, values, bias,
    w_recv, w_swap, w_send, r_recv, own_sem, act_recv, act_send,
    px_recv, px_send, out_recv, out_send, in_sem,
    far_out, far_in, far_keep, far_stage, far_recv,
):
    group, dp, core = lax.axis_index("groups"), lax.axis_index("dp"), lax.axis_index("tensor")
    z, y = dp // 2, dp % 2
    x = group % 2
    cousin = group + 1 - 2 * x
    other = 1 - core
    half = z // 2
    inner = z % 2 != half
    outer = jnp.logical_not(inner)
    zp = z + 1 - 2 * (z % 2)
    zm = jnp.where(inner, line - 1 - z, z)
    peer = z * 2 + 1 - y
    part, cols = w_ref.shape
    tokens, wide = q_ref.shape
    chunks = part // CHUNK
    unit = cols // 2
    lane = unit // 2
    tall = 2 * CHUNK
    rows_mine = tokens // 2
    steps = wide // 256
    step_cols = wide // steps
    heads_per_step = step_cols // HEAD_SIZE
    near, far = steps * OUTER_ZY // 8, steps * INNER_ZY // 8

    def remote(src, dst, send, recv, where):
        return pltpu.make_async_remote_copy(
            src_ref=src, dst_ref=dst, send_sem=send, recv_sem=recv,
            device_id=where, device_id_type=pl.DeviceIdType.MESH,
        )

    def loop(low, high, act_on):
        lax.fori_loop(low, high, lambda k, carry: (act_on(k), carry)[1], 0)

    def rows(k):
        return pl.ds(pl.multiple_of(k * CHUNK, CHUNK), CHUNK)

    cached = table_ref.shape[1] * PAGE_TOKENS

    loads = [
        pltpu.make_async_copy(kp_hbm, kp_ref, in_sem.at[0]),
        pltpu.make_async_copy(vp_hbm, vp_ref, in_sem.at[1]),
        pltpu.make_async_copy(fk_hbm, keys.at[cached:], in_sem.at[2]),
        pltpu.make_async_copy(fv_hbm, values.at[cached:], in_sem.at[3]),
        pltpu.make_async_copy(q_hbm, q_ref, in_sem.at[4]),
    ]
    for copy in loads:
        copy.start()

    barrier = pltpu.get_barrier_semaphore()

    def greet(where):
        pl.semaphore_signal(barrier, inc=1, device_id=where, device_id_type=pl.DeviceIdType.MESH)

    greet((group, dp, other))
    for chip in (peer, zp * 2 + y, zp * 2 + 1 - y):
        greet((group, chip, core))
        greet((group, chip, other))

    @pl.when(inner)
    def _():
        greet((cousin, dp, core))
        greet((group, zm * 2 + y, core))

    pl.semaphore_wait(barrier, 7 + jnp.where(inner, 2, 0))

    half_cols = pl.ds(pl.multiple_of(x * unit, 128), unit)
    deep = chunks // 2

    def patch(k):
        return (pl.ds(pl.multiple_of(k % deep * tall, tall), tall),
                pl.ds(pl.multiple_of(k // deep * lane, 128), lane))

    def mid_own(k):
        return remote(
            w_ref.at[rows(k), half_cols], wall.at[1, x, rows(k)],
            w_send.at[0], w_recv.at[0, k], (group, zm * 2 + y, core),
        )

    def to_relay(k):
        return remote(
            w_ref.at[patch(k)[0], pl.ds(pl.multiple_of(x * unit + k // deep * lane, 128), lane)], relay.at[patch(k)],
            w_send.at[0], r_recv.at[k], (group, zp * 2 + y, core),
        )

    def mid_relay(k):
        return remote(
            relay.at[patch(k)], wall.at[2, x, *patch(k)],
            w_send.at[1], w_recv.at[1, k], (group, zm * 2 + y, core),
        )

    def side(s, k):
        if s == 1:
            ref, sem = wall.at[s, x, rows(k)], w_swap.at[0]
        else:
            ref, sem = wall.at[s, x, *patch(k)], w_swap.at[1 + k // deep]
        return remote(ref, ref, w_send.at[s + 1], sem, (cousin, dp, core))

    def swapped(ref, n):
        remote(ref, ref, w_send.at[2], w_swap.at[n], (cousin, dp, core)).wait_recv()

    def near_swapped():
        swapped(wall.at[1, 1 - x], 0)

    def far_swapped(v):
        swapped(wall.at[2, 1 - x, :, v * lane:(v + 1) * lane], 1 + v)

    def relay_on(k):
        to_relay(k).wait_recv()
        mid_relay(k).start()

    def side_on(s, k):
        (mid_own(k) if s == 1 else mid_relay(k)).wait_recv()
        side(s, k).start()

    def own_copy(u):
        return pltpu.make_async_copy(
            w_ref.at[:, u * unit:(u + 1) * unit], wall.at[0, u], own_sem.at[u]
        )

    @pl.when(inner)
    def _():
        loop(0, chunks, lambda k: mid_own(k).start())

    @pl.when(outer)
    def _():
        to_relay(0).start()

    own_copy(0).start()
    own_copy(1).start()

    length = len_ref[dp]
    position = lax.broadcasted_iota(jnp.int32, (tokens, cached), 1)
    bias[:, :cached] = jnp.where(position < length, 0.0, MASKED)
    bias[:, cached:] = jnp.where(
        lax.broadcasted_iota(jnp.int32, (tokens, tokens), 1)
        <= lax.broadcasted_iota(jnp.int32, (tokens, tokens), 0),
        0.0, MASKED,
    )
    for copy in loads:
        copy.wait()
    for j in range(table_ref.shape[1]):
        page = table_ref[0, j]
        keys[j * PAGE_TOKENS:(j + 1) * PAGE_TOKENS, :] = kp_ref[page]
        values[j * PAGE_TOKENS:(j + 1) * PAGE_TOKENS, :] = vp_ref[page]

    def act_at(slot, i):
        return act.at[slot, :, pl.ds(pl.multiple_of(i * step_cols, step_cols), step_cols)]

    def act_y(i):
        return remote(act_at(0, i), act_at(1, i), act_send.at[0], act_recv.at[1, i],
                      (group, peer, core))

    def act_z(i):
        return remote(act_at(0, i), act_at(2, i), act_send.at[1], act_recv.at[0, i],
                      (group, zp * 2 + y, core))

    def on_y(i):
        return remote(act_at(2, i), act_at(3, i), act_send.at[2], act_recv.at[1, steps],
                      (group, peer, core))

    def on_z(i):
        return remote(act_at(1, i), act_at(3, i), act_send.at[3], act_recv.at[1, steps],
                      (group, zp * 2 + y, core))

    over_y = jnp.where(inner, near, far)
    over_z = jnp.where(inner, far, near)

    def from_y(i):
        act_y(i).wait_recv()

        @pl.when(i >= over_z)
        def _():
            on_z(i).start()

    def from_z(i):
        act_z(i).wait_recv()

        @pl.when(i < over_y)
        def _():
            on_y(i).start()

    def attention_step(i):
        kv = (i * heads_per_step) // QUERY_GROUP
        kv_cols = pl.ds(pl.multiple_of(kv * HEAD_SIZE, HEAD_SIZE), HEAD_SIZE)
        for n in range(heads_per_step):
            start = pl.multiple_of((i * heads_per_step + n) * HEAD_SIZE, HEAD_SIZE)
            q = q_ref[:, pl.ds(start, HEAD_SIZE)]
            scores = lax.dot_general(
                q, keys[:, kv_cols], (((1,), (1,)), ((), ())), preferred_element_type=jnp.float32
            )
            scores = scores * SCALE + bias[...]
            weights = jnp.exp2(scores - jnp.max(scores, axis=-1, keepdims=True))
            total = jnp.sum(weights, axis=-1, keepdims=True)
            weighted = jnp.dot(
                weights.astype(jnp.bfloat16), values[:, kv_cols], preferred_element_type=jnp.float32
            )
            act[0, :, pl.ds(start, HEAD_SIZE)] = (weighted / total).astype(jnp.bfloat16)
        act_y(i).start()
        act_z(i).start()

        @pl.when(jnp.logical_and(outer, i % 2 == 1))
        def _():
            to_relay((i + 1) // 2).start()

        @pl.when(jnp.logical_and(inner, jnp.logical_and(i >= 3, i % 2 == 1)))
        def _():
            side_on(1, (i - 3) // 2)

        @pl.when(jnp.logical_and(inner, i == 3))
        def _():
            relay_on(0)

    loop(0, steps, attention_step)

    @pl.when(outer)
    def _():
        loop(steps // 2 + 1, chunks, lambda k: to_relay(k).start())

    def shard_z(s):
        return jnp.where(s == 0, z, zm)

    def task(s, u, slot):
        return (s * 2 + u) * 4 + slot

    def swap(t):
        return remote(px_out.at[t], px_in.at[t], px_send.at[0], px_recv.at[t], (group, dp, other))

    def place(s, u):
        zs = shard_z(s)
        to = zs // 2
        column = (zs * 2 + y - to * line) * cols + u * unit
        ref = out_ref.at[pl.ds(pl.multiple_of(core * rows_mine, rows_mine), rows_mine),
                         pl.ds(pl.multiple_of(column, 128), unit)]
        return to, ref

    def out_copy(s, u, slot):
        to, ref = place(s, u)
        t = task(s, u, slot)
        zd = jnp.where(slot >= 2, zp, z)
        yd = jnp.where(slot % 2 == 1, 1 - y, y)
        return remote(stage.at[t], ref, out_send.at[0], out_recv.at[0], (group, zd * 2 + yd, to))

    def stays(s, slot):
        return jnp.logical_and(slot == 0, shard_z(s) // 2 == core)

    def begin(s, u, slot):
        t = task(s, u, slot)
        keep[t] = jnp.dot(act[slot], wall[s, u], preferred_element_type=jnp.float32)
        start = pl.multiple_of(other * rows_mine, rows_mine)
        px_out[t] = keep[t, pl.ds(start, rows_mine), :].astype(jnp.bfloat16)
        swap(t).start()

    def finish(s, u, slot):
        t = task(s, u, slot)
        swap(t).wait_recv()
        start = pl.multiple_of(core * rows_mine, rows_mine)
        stage[t] = (keep[t, pl.ds(start, rows_mine), :] + px_in[t].astype(jnp.float32)).astype(jnp.bfloat16)

        @pl.when(stays(s, slot))
        def _():
            to, ref = place(s, u)
            pltpu.make_async_copy(stage.at[t], ref, out_recv.at[0]).start()

        @pl.when(jnp.logical_not(stays(s, slot)))
        def _():
            out_copy(s, u, slot).start()

    def strip(w):
        return jnp.where(w % 2 == 0, x, 1 - x), w // 2

    def far_swap(w, p):
        pair = pl.ds(p * 2, 2)
        return remote(far_out.at[w, pair], far_in.at[w, pair], px_send.at[1], far_recv.at[w, p],
                      (group, dp, other))

    def far_begin(w, p):
        u, v = strip(w)
        pair = pl.ds(p * 2, 2)
        far_keep[w, pair] = jnp.dot(
            act[pair].reshape(2 * tokens, wide), wall[2, u, :, pl.ds(pl.multiple_of(v * lane, 128), lane)],
            preferred_element_type=jnp.float32,
        ).reshape(2, tokens, lane)
        start = pl.multiple_of(other * rows_mine, rows_mine)
        far_out[w, pair] = far_keep[w, pair, pl.ds(start, rows_mine), :].astype(jnp.bfloat16)
        far_swap(w, p).start()

    def far_place(w):
        u, v = strip(w)
        zs = (line - 1) * (1 - half)
        to = zs // 2
        column = (zs * 2 + y - to * line) * cols + u * unit + v * lane
        ref = out_ref.at[pl.ds(pl.multiple_of(core * rows_mine, rows_mine), rows_mine),
                         pl.ds(pl.multiple_of(column, 128), lane)]
        return to, ref

    def far_copy(w, slot):
        to, ref = far_place(w)
        zd = jnp.where(slot >= 2, zp, z)
        yd = jnp.where(slot % 2 == 1, 1 - y, y)
        return remote(far_stage.at[w, slot], ref, out_send.at[1], out_recv.at[0], (group, zd * 2 + yd, to))

    def far_stays(slot):
        return jnp.logical_and(slot == 0, 1 - half == core)

    def far_finish(w, p):
        far_swap(w, p).wait_recv()
        pair = pl.ds(p * 2, 2)
        start = pl.multiple_of(core * rows_mine, rows_mine)
        far_stage[w, pair] = (
            far_keep[w, pair, pl.ds(start, rows_mine), :] + far_in[w, pair].astype(jnp.float32)
        ).astype(jnp.bfloat16)
        far_copy(w, p * 2 + 1).start()

        @pl.when(far_stays(p * 2))
        def _():
            to, ref = far_place(w)
            pltpu.make_async_copy(far_stage.at[w, p * 2], ref, out_recv.at[0]).start()

        @pl.when(jnp.logical_not(far_stays(p * 2)))
        def _():
            far_copy(w, p * 2).start()

    own_copy(0).wait()
    own_copy(1).wait()

    def run(count, kinds, duties):
        def each(n, what):
            for holds, which, acts in kinds:
                @pl.when(holds(n))
                def _():
                    acts[what](*which(n))

        def one(n):
            for at, todo in duties.items():
                @pl.when(n == at)
                def _():
                    for act_now in todo:
                        act_now()

            @pl.when(n < count)
            def _():
                each(n, 0)

            @pl.when(n > 0)
            def _():
                each(n - 1, 1)

        loop(0, count + 1, one)

    def corner_landed():
        remote(act.at[2], act.at[3], act_send.at[2], act_recv.at[1, steps], (group, peer, core)).wait_recv()

    P = functools.partial
    near_tasks = (begin, finish)
    far_tasks = (far_begin, far_finish)

    @pl.when(outer)
    def _():
        run(8, [(lambda n: n >= 0, lambda n: (0, n % 2, n // 2), near_tasks)], {
            0: [lambda: loop(0, steps, from_z)],
            2: [lambda: loop(0, steps, from_y)],
            6: [corner_landed],
        })

    @pl.when(inner)
    def _():
        def is_far(n):
            return jnp.logical_or(n >= 18, jnp.logical_and(n >= 12, n < 14))

        def near_which(n):
            m = jnp.where(n < 12, n, n - 2)
            return (m % 4) // 2, m % 2, m // 4

        def far_which(n):
            late = n >= 20
            return (jnp.where(n < 14, n - 12, jnp.where(late, 2 + (n - 20) // 2, n - 18)),
                    jnp.where(n < 14, 0, jnp.where(late, 1 - n % 2, 1)))

        kinds = [(lambda n: jnp.logical_not(is_far(n)), near_which, near_tasks), (is_far, far_which, far_tasks)]
        run(24, kinds, {
            0: [P(side_on, 1, 3), P(relay_on, 1)],
            1: [P(side_on, 1, 4), P(from_z, 0), P(from_z, 1), P(from_z, 2)],
            2: [P(side_on, 1, 5), P(from_z, 3), P(side_on, 1, 6), P(relay_on, 2), P(side_on, 1, 7), P(from_z, 4),
                lambda: loop(0, steps, from_y), P(side_on, 2, 0), P(from_z, 5),
                near_swapped],
            3: [P(relay_on, 3)],
            4: [P(side_on, 2, 1)],
            6: [P(from_z, 6), P(side_on, 2, 2)],
            8: [P(from_z, 7), P(side_on, 2, 3)],
            9: [P(relay_on, 4)],
            11: [P(relay_on, 5)],
            12: [P(side_on, 2, 4)],
            13: [P(far_swapped, 0)],
            14: [P(relay_on, 6), P(side_on, 2, 5), P(relay_on, 7), corner_landed, P(side_on, 2, 6)],
            15: [P(side_on, 2, 7)],
            22: [P(far_swapped, 1)],
        })

    def sent(ref, sem):
        remote(ref, ref, sem, sem, (group, dp, other)).wait_send()

    def sent_if(holds, ref, sem):
        @pl.when(holds)
        def _():
            sent(ref, sem)

    sent(act.at[0], act_send.at[0])
    sent(act.at[0], act_send.at[1])
    unit_ref = wall.at[0, 0]
    sent(unit_ref, w_send.at[0])
    far_goes = jnp.logical_and(inner, core == half)
    far_mate = jnp.logical_and(inner, core != half)
    sent_if(inner, stage.at[0:14], out_send.at[0])
    sent_if(jnp.logical_and(outer, core == half), stage.at[0:6], out_send.at[0])
    sent_if(jnp.logical_and(outer, core != half), stage.at[0:8], out_send.at[0])
    sent_if(inner, px_out, px_send.at[0])
    sent_if(outer, px_out.at[0:8], px_send.at[0])
    sent_if(inner, far_out, px_send.at[1])
    sent_if(far_goes, far_stage, out_send.at[1])
    sent_if(far_mate, far_stage.at[0:3], out_send.at[1])
    for n in range(1, 4):
        sent_if(inner, unit_ref, w_send.at[n])

    def columns(low, high):
        return act.at[0, :, low * step_cols:high * step_cols]

    for holds, y_count, z_count in ((inner, near, steps - far), (outer, far, steps - near)):
        if y_count:
            sent_if(holds, columns(0, y_count), act_send.at[2])
        if z_count:
            sent_if(holds, columns(0, z_count), act_send.at[3])

    remote(out_ref, out_ref, out_recv.at[0], out_recv.at[0], (group, dp, other)).wait_recv()


def square_program(line, queries, fresh_keys, fresh_values, key_pages, value_pages, table, lengths, weight):
    tokens, wide = queries.shape
    part, cols = weight.shape
    chunks = part // CHUNK
    steps = wide // 256
    unit = cols // 2
    span = table.shape[1] * PAGE_TOKENS + tokens
    kv_width = fresh_keys.shape[1]
    hbm = pl.BlockSpec(memory_space=pl.ANY)
    smem = pl.BlockSpec(memory_space=pltpu.SMEM)
    dma = pltpu.SemaphoreType.DMA
    bf16, f32 = jnp.bfloat16, jnp.float32
    heads = wide // HEAD_SIZE
    flops = 4 * heads * tokens * span * HEAD_SIZE + 2 * 24 * tokens * part * unit
    return pl.pallas_call(
        functools.partial(square_kernel, line),
        out_shape=jax.ShapeDtypeStruct((tokens, line * cols), bf16),
        in_specs=[hbm, hbm, hbm, hbm, hbm, smem, smem, hbm],
        out_specs=hbm,
        scratch_shapes=[
            pltpu.VMEM(queries.shape, bf16),
            pltpu.VMEM(key_pages.shape, bf16),
            pltpu.VMEM(value_pages.shape, bf16),
            pltpu.VMEM((4, tokens, wide), bf16),
            pltpu.VMEM((3, 2, part, unit), bf16),
            pltpu.VMEM((part, unit), bf16),
            pltpu.VMEM((16, tokens // 2, unit), bf16),
            pltpu.VMEM((16, tokens // 2, unit), bf16),
            pltpu.VMEM((16, tokens, unit), f32),
            pltpu.VMEM((16, tokens // 2, unit), bf16),
            pltpu.VMEM((span, kv_width), bf16),
            pltpu.VMEM((span, kv_width), bf16),
            pltpu.VMEM((tokens, span), f32),
            dma((2, chunks)),
            dma((3,)),
            dma((4,)),
            dma((chunks,)),
            dma((2,)),
            dma((2, steps + 1)),
            dma((4,)),
            dma((16,)),
            dma((2,)),
            dma((1,)),
            dma((2,)),
            dma((5,)),
            pltpu.VMEM((4, 4, tokens // 2, unit // 2), bf16),
            pltpu.VMEM((4, 4, tokens // 2, unit // 2), bf16),
            pltpu.VMEM((4, 4, tokens, unit // 2), f32),
            pltpu.VMEM((4, 4, tokens // 2, unit // 2), bf16),
            dma((4, 2)),
        ],
        compiler_params=pltpu.CompilerParams(
            collective_id=0, has_side_effects=True, vmem_limit_bytes=60 * 1024 * 1024
        ),
        cost_estimate=pl.CostEstimate(
            flops=flops, bytes_accessed=8 * 1024 * 1024, transcendentals=heads * tokens * span
        ),
    )(queries, fresh_keys, fresh_values, key_pages, value_pages, table, lengths, weight)


def program_of(line):
    return square_program if line == 4 else shards_program


def solution(mesh):
    return jax.shard_map(
        functools.partial(program_of(mesh.shape["dp"] // 2), mesh.shape["dp"] // 2),
        mesh=mesh,
        in_specs=(
            P(("groups", "dp"), "tensor"),
            P(("groups", "dp"), "tensor"),
            P(("groups", "dp"), "tensor"),
            P(("groups", "dp"), None, "tensor"),
            P(("groups", "dp"), None, "tensor"),
            P(("groups", "dp"), None),
            P("groups"),
            P("tensor", "dp"),
        ),
        out_specs=P(("groups", "dp"), "tensor"),
        check_vma=False,
    )
```

```python
import functools

import jax
import jax.numpy as jnp
from jax import lax
from jax.experimental import pallas as pl
from jax.experimental.pallas import tpu as pltpu
from jax.sharding import PartitionSpec as P

HEAD_SIZE = 128
QUERY_GROUP = 8
PAGE_TOKENS = 128
CHUNK = 256
OUTER_ZY = 8
INNER_ZY = 5
SCALE = HEAD_SIZE ** (-0.5) * 1.4426950408889634
MASKED = -1e30


def kernel(
    line, q_ref, fk_ref, fv_ref, kp_ref, vp_ref, table_ref, len_ref, w_ref, out_ref,
    wbuf, act, stage, keys, values, bias,
    w_recv, w_next, w_side, own_send, act_recv, act_send, act_fwd, out_send, out_recv,
):
    group, dp, core = lax.axis_index("groups"), lax.axis_index("dp"), lax.axis_index("tensor")
    z, y = dp // 2, dp % 2
    half = group % 2
    cousin = group + 1 - 2 * half
    other = 1 - core
    peer = z * 2 + 1 - y
    shards = line // 2
    part, cols = w_ref.shape
    tokens = q_ref.shape[0]
    per_core = part // CHUNK
    per_half = per_core // 2
    own_core = z // shards
    own_slot = z - own_core * shards
    wide = act.shape[2] // 2
    step_cols = wide // per_core
    heads_per_step = step_cols // HEAD_SIZE
    heads_per_kv = QUERY_GROUP
    tile = min(cols, 256)
    tiles = cols // tile

    def remote(src, dst, send, recv, where):
        return pltpu.make_async_remote_copy(
            src_ref=src, dst_ref=dst, send_sem=send, recv_sem=recv,
            device_id=where, device_id_type=pl.DeviceIdType.MESH,
        )

    def rows(k):
        return pl.ds(pl.multiple_of(k * CHUNK, CHUNK), CHUNK)

    barrier = pltpu.get_barrier_semaphore()

    def greet(where):
        pl.semaphore_signal(barrier, inc=1, device_id=where, device_id_type=pl.DeviceIdType.MESH)

    greet((group, dp, other))
    greet((cousin, dp, core))
    greet((group, peer, core))

    @pl.when(z > 0)
    def _():
        greet((group, dp - 2, core))
        greet((group, dp - 2, other))

    @pl.when(z < line - 1)
    def _():
        greet((group, dp + 2, core))
        greet((group, dp + 2, other))

    neighbours = jnp.where(z > 0, 2, 0) + jnp.where(z < line - 1, 2, 0)
    pl.semaphore_wait(barrier, 3 + neighbours)

    def own_copy(k, side):
        slab = core * per_core + k
        where = (group, dp + 2 * side, own_core) if side else (group, dp, other)
        return remote(
            w_ref.at[rows(k)], wbuf.at[own_slot, rows(slab)],
            own_send.at[side + 1, k], w_recv.at[own_slot, slab], where,
        )

    def own_local(k):
        slab = core * per_core + k
        return pltpu.make_async_copy(
            w_ref.at[rows(k)], wbuf.at[own_slot, rows(slab)], w_recv.at[own_slot, slab]
        )

    def each_own(act_on):
        def one(j, carry):
            k = half * per_half + j

            @pl.when(z > 0)
            def _():
                act_on(own_copy(k, -1))

            @pl.when(z < line - 1)
            def _():
                act_on(own_copy(k, 1))

            return carry

        lax.fori_loop(0, per_half, one, 0)

        @pl.when(core != own_core)
        def _():
            lax.fori_loop(0, per_core, lambda k, carry: (act_on(own_copy(k, 0)), carry)[1], 0)

    each_own(lambda copy: copy.start())

    @pl.when(core == own_core)
    def _():
        lax.fori_loop(0, per_core, lambda k, carry: (own_local(k).start(), carry)[1], 0)

    def slab_of(i, which):
        return (i % 2) * per_core + which * per_half + i // 2

    def landed(slot, slab):
        remote(
            wbuf.at[slot, rows(slab)], wbuf.at[slot, rows(slab)],
            w_next.at[slot, slab], w_recv.at[slot, slab], (group, dp, other),
        ).wait_recv()

    def next_copy(slot, slab, step):
        return remote(
            wbuf.at[slot, rows(slab)], wbuf.at[slot, rows(slab)],
            w_next.at[slot, slab], w_recv.at[slot, slab], (group, dp + 2 * step, core),
        )

    def side_copy(slot, slab):
        return remote(
            wbuf.at[slot, rows(slab)], wbuf.at[slot, rows(slab)],
            w_side.at[slot, slab], w_recv.at[slot, slab], (cousin, dp, core),
        )

    def pass_on(slot, origin, i):
        slab = slab_of(i, half)
        landed(slot, slab)

        @pl.when(jnp.logical_and(origin < z, z < line - 1))
        def _():
            next_copy(slot, slab, 1).start()

        @pl.when(jnp.logical_and(origin > z, z > 0))
        def _():
            next_copy(slot, slab, -1).start()

        side_copy(slot, slab).start()

    length = len_ref[dp]
    cached = table_ref.shape[1] * PAGE_TOKENS
    for j in range(table_ref.shape[1]):
        page = table_ref[0, j]
        keys[j * PAGE_TOKENS:(j + 1) * PAGE_TOKENS, :] = kp_ref[page]
        values[j * PAGE_TOKENS:(j + 1) * PAGE_TOKENS, :] = vp_ref[page]
    keys[cached:, :] = fk_ref[...]
    values[cached:, :] = fv_ref[...]
    position = lax.broadcasted_iota(jnp.int32, (tokens, cached), 1)
    bias[:, :cached] = jnp.where(position < length, 0.0, MASKED)
    bias[:, cached:] = jnp.where(
        lax.broadcasted_iota(jnp.int32, (tokens, tokens), 1)
        <= lax.broadcasted_iota(jnp.int32, (tokens, tokens), 0),
        0.0, MASKED,
    )

    def act_cols(slab):
        return pl.ds(pl.multiple_of(slab * step_cols, step_cols), step_cols)

    def act_copy(i, to_peer):
        slab = core * per_core + i
        src = act.at[0, :, act_cols(slab)]
        if to_peer:
            return remote(src, act.at[1, :, act_cols(slab)], act_send.at[1, i],
                          act_recv.at[1, slab], (group, peer, core))
        return remote(src, src, act_send.at[0, i], act_recv.at[0, slab], (group, dp, other))

    def act_forward(i):
        slab = core * per_core + i
        ref = act.at[1, :, act_cols(slab)]
        return remote(ref, ref, act_fwd.at[i], act_recv.at[1, slab], (group, dp, other))

    def act_landed(block, slab):
        ref = act.at[block, :, act_cols(slab)]
        remote(ref, ref, act_fwd.at[0], act_recv.at[block, slab], (group, dp, other)).wait_recv()

    def relay(i):
        act_landed(1, core * per_core + i)
        act_forward(i).start()

    lag = 2

    def attention_step(i, carry):
        kv = (i * heads_per_step) // heads_per_kv
        kv_cols = pl.ds(pl.multiple_of(kv * HEAD_SIZE, HEAD_SIZE), HEAD_SIZE)
        for n in range(heads_per_step):
            head = i * heads_per_step + n
            q = q_ref[:, pl.ds(pl.multiple_of(head * HEAD_SIZE, HEAD_SIZE), HEAD_SIZE)]
            scores = lax.dot_general(
                q, keys[:, kv_cols], (((1,), (1,)), ((), ())), preferred_element_type=jnp.float32
            )
            scores = scores * SCALE + bias[...]
            weights = jnp.exp2(scores - jnp.max(scores, axis=-1, keepdims=True))
            total = jnp.sum(weights, axis=-1, keepdims=True)
            weighted = jnp.dot(
                weights.astype(jnp.bfloat16), values[:, kv_cols], preferred_element_type=jnp.float32
            )
            start = core * wide + head * HEAD_SIZE
            act[0, :, pl.ds(pl.multiple_of(start, HEAD_SIZE), HEAD_SIZE)] = (
                weighted / total
            ).astype(jnp.bfloat16)
        act_copy(i, True).start()
        act_copy(i, False).start()
        for side in (-1, 1):
            origin = z + side

            @pl.when(jnp.logical_and(
                jnp.logical_and(origin >= core * shards, origin < (core + 1) * shards), True))
            def _():
                pass_on(origin - core * shards, origin, i)

        @pl.when(i >= lag)
        def _():
            relay(i - lag)

        return carry

    lax.fori_loop(0, per_core, attention_step, 0)
    for i in range(per_core - lag, per_core):
        relay(i)

    def origin_of(p):
        low = core * shards
        inside = low + (z - low + p + shards * line) % shards
        return jnp.where(z < low, low + p, jnp.where(z >= low + shards, low + shards - 1 - p, inside))

    def out_cols(origin, n):
        start = (origin * 2 + y - core * 2 * shards) * cols + n * tile
        return pl.ds(pl.multiple_of(start, 128), tile)

    def out_copy(slot, n, column):
        return remote(
            stage.at[slot, n], out_ref.at[:, column], out_send.at[slot, n],
            out_recv.at[slot, n], (group, peer, core),
        )

    def product(block, slot, n):
        return jnp.dot(
            act[block], wbuf[slot, :, pl.ds(pl.multiple_of(n * tile, 128), tile)],
            preferred_element_type=jnp.float32,
        ).astype(jnp.bfloat16)

    def piece(origin, m):
        slot = origin - core * shards
        n = m % tiles
        column = out_cols(origin, n)

        @pl.when(m < tiles)
        def _():
            stage[slot, n] = product(1, slot, n)
            out_copy(slot, n, column).start()

        @pl.when(m >= tiles)
        def _():
            out_ref[:, column] = product(0, slot, n)

    def rest_landed(origin):
        slot = origin - core * shards

        def one(i, carry):
            landed(slot, slab_of(i, 1 - half))

            @pl.when(origin == z)
            def _():
                landed(slot, slab_of(i, half))

            return carry

        lax.fori_loop(0, per_core, one, 0)

    def acts_landed():
        def one(i, carry):
            act_landed(0, other * per_core + i)
            act_landed(1, other * per_core + i)
            return carry

        lax.fori_loop(0, per_core, one, 0)

    def shard_step(p, carry):
        origin = origin_of(p)
        before = origin_of(jnp.maximum(p - 1, 0))

        def chunk_step(i, inner):
            @pl.when(jnp.logical_or(origin > z + 1, origin < z - 1))
            def _():
                pass_on(origin - core * shards, origin, i)

            return inner

        lax.fori_loop(0, per_core, chunk_step, 0)

        @pl.when(p > 0)
        def _():
            @pl.when(p == 1)
            def _():
                acts_landed()

            rest_landed(before)
            lax.fori_loop(0, 2 * tiles, lambda m, inner: (piece(before, m), inner)[1], 0)

        return carry

    lax.fori_loop(0, shards, shard_step, 0)
    if shards == 1:
        acts_landed()
    last = origin_of(shards - 1)
    rest_landed(last)
    lax.fori_loop(0, 2 * tiles, lambda m, carry: (piece(last, m), carry)[1], 0)

    def finish(slot, carry):
        origin = core * shards + slot
        for n in range(tiles):
            start = (origin * 2 + 1 - y - core * 2 * shards) * cols + n * tile
            copy = out_copy(slot, n, pl.ds(pl.multiple_of(start, 128), tile))
            copy.wait_recv()
            copy.wait_send()

        @pl.when(origin != z)
        def _():
            def one(i, inner):
                slab = slab_of(i, half)

                @pl.when(jnp.logical_and(origin < z, z < line - 1))
                def _():
                    next_copy(slot, slab, 1).wait_send()

                @pl.when(jnp.logical_and(origin > z, z > 0))
                def _():
                    next_copy(slot, slab, -1).wait_send()

                side_copy(slot, slab).wait_send()
                return inner

            lax.fori_loop(0, per_core, one, 0)

        return carry

    lax.fori_loop(0, shards, finish, 0)

    def acts_sent(i, carry):
        act_copy(i, True).wait_send()
        act_copy(i, False).wait_send()
        act_forward(i).wait_send()
        return carry

    lax.fori_loop(0, per_core, acts_sent, 0)
    each_own(lambda copy: copy.wait_send())


def shards_program(line, queries, fresh_keys, fresh_values, key_pages, value_pages, table, lengths, weight):
    tokens, wide = queries.shape
    part, cols = weight.shape
    per_core = part // CHUNK
    shards = line // 2
    tile = min(cols, 256)
    tiles = cols // tile
    span = table.shape[1] * PAGE_TOKENS + tokens
    kv_width = fresh_keys.shape[1]
    out_width = 2 * shards * cols
    vmem = pl.BlockSpec(memory_space=pltpu.VMEM)
    smem = pl.BlockSpec(memory_space=pltpu.SMEM)
    dma = pltpu.SemaphoreType.DMA
    heads = wide // HEAD_SIZE
    flops = 4 * heads * tokens * span * HEAD_SIZE + 2 * 2 * tokens * 2 * part * shards * cols
    return pl.pallas_call(
        functools.partial(kernel, line),
        out_shape=jax.ShapeDtypeStruct((tokens, out_width), jnp.bfloat16),
        in_specs=[vmem, vmem, vmem, vmem, vmem, smem, smem, pl.BlockSpec(memory_space=pl.ANY)],
        out_specs=vmem,
        scratch_shapes=[
            pltpu.VMEM((shards, 2 * part, cols), jnp.bfloat16),
            pltpu.VMEM((2, tokens, 2 * wide), jnp.bfloat16),
            pltpu.VMEM((shards, tiles, tokens, tile), jnp.bfloat16),
            pltpu.VMEM((span, kv_width), jnp.bfloat16),
            pltpu.VMEM((span, kv_width), jnp.bfloat16),
            pltpu.VMEM((tokens, span), jnp.float32),
            dma((shards, 2 * per_core)),
            dma((shards, 2 * per_core)),
            dma((shards, 2 * per_core)),
            dma((3, per_core)),
            dma((2, 2 * per_core)),
            dma((2, per_core)),
            dma((per_core,)),
            dma((shards, tiles)),
            dma((shards, tiles)),
        ],
        compiler_params=pltpu.CompilerParams(
            collective_id=0, has_side_effects=True, vmem_limit_bytes=60 * 1024 * 1024
        ),
        cost_estimate=pl.CostEstimate(
            flops=flops, bytes_accessed=8 * 1024 * 1024, transcendentals=heads * tokens * span
        ),
    )(queries, fresh_keys, fresh_values, key_pages, value_pages, table, lengths, weight)


def square_kernel(
    line, q_hbm, fk_hbm, fv_hbm, kp_hbm, vp_hbm, table_ref, len_ref, w_ref, out_ref,
    q_ref, kp_ref, vp_ref, act, wall, far_wall, relay, px_out, px_in, keep, stage, keys, values, bias,
    w_recv, w_swap, w_send, r_recv, own_sem, act_recv, act_send,
    px_recv, px_send, out_recv, out_send, in_sem,
    far_out, far_in, far_keep, far_stage, far_recv,
):
    group, dp, core = lax.axis_index("groups"), lax.axis_index("dp"), lax.axis_index("tensor")
    z, y = dp // 2, dp % 2
    x = group % 2
    cousin = group + 1 - 2 * x
    other = 1 - core
    half = z // 2
    inner = z % 2 != half
    outer = jnp.logical_not(inner)
    zp = z + 1 - 2 * (z % 2)
    zm = jnp.where(inner, line - 1 - z, z)
    peer = z * 2 + 1 - y
    part, cols = w_ref.shape
    tokens, wide = q_ref.shape
    chunks = part // CHUNK
    unit = cols // 2
    lane = unit // 2
    tall = 2 * CHUNK
    rows_mine = tokens // 2
    steps = wide // 256
    step_cols = wide // steps
    heads_per_step = step_cols // HEAD_SIZE
    near, far = steps * OUTER_ZY // 8, steps * INNER_ZY // 8

    def remote(src, dst, send, recv, where):
        return pltpu.make_async_remote_copy(
            src_ref=src, dst_ref=dst, send_sem=send, recv_sem=recv,
            device_id=where, device_id_type=pl.DeviceIdType.MESH,
        )

    def loop(low, high, act_on):
        lax.fori_loop(low, high, lambda k, carry: (act_on(k), carry)[1], 0)

    def rows(k):
        return pl.ds(pl.multiple_of(k * CHUNK, CHUNK), CHUNK)

    cached = table_ref.shape[1] * PAGE_TOKENS

    loads = [
        pltpu.make_async_copy(kp_hbm, kp_ref, in_sem.at[0]),
        pltpu.make_async_copy(vp_hbm, vp_ref, in_sem.at[1]),
        pltpu.make_async_copy(fk_hbm, keys.at[cached:], in_sem.at[2]),
        pltpu.make_async_copy(fv_hbm, values.at[cached:], in_sem.at[3]),
        pltpu.make_async_copy(q_hbm, q_ref, in_sem.at[4]),
    ]
    for copy in loads:
        copy.start()

    barrier = pltpu.get_barrier_semaphore()

    def greet(where):
        pl.semaphore_signal(barrier, inc=1, device_id=where, device_id_type=pl.DeviceIdType.MESH)

    greet((group, dp, other))
    for chip in (peer, zp * 2 + y, zp * 2 + 1 - y):
        greet((group, chip, core))
        greet((group, chip, other))

    @pl.when(inner)
    def _():
        greet((cousin, dp, core))
        greet((group, zm * 2 + y, core))

    pl.semaphore_wait(barrier, 7 + jnp.where(inner, 2, 0))

    half_cols = pl.ds(pl.multiple_of(x * unit, 128), unit)
    half_lane = pl.ds(pl.multiple_of(x * lane, 128), lane)
    rest_cols = pl.ds(pl.multiple_of((1 - x) * unit, 128), unit)
    rest_lane = pl.ds(pl.multiple_of((1 - x) * lane, 128), lane)
    deep = chunks // 2
    pieces = deep + chunks

    def patch(k):
        if isinstance(k, jax.Array) or k < deep:
            return 0, pl.ds(pl.multiple_of(k * tall, tall), tall)
        return 1, pl.ds((k - deep) * CHUNK, CHUNK)

    def mid_own(k):
        return remote(
            w_ref.at[rows(k), half_cols], wall.at[1, rows(k), half_cols],
            w_send.at[0], w_recv.at[0, k], (group, zm * 2 + y, core),
        )

    def to_relay(k):
        v, part_rows = patch(k)
        column = pl.ds(pl.multiple_of(x * unit + v * lane, 128), lane)
        return remote(
            w_ref.at[part_rows, column], relay.at[v, part_rows],
            w_send.at[0], r_recv.at[k], (group, zp * 2 + y, core),
        )

    def mid_relay(k):
        v, part_rows = patch(k)
        return remote(
            relay.at[v, part_rows], far_wall.at[v, part_rows, half_lane],
            w_send.at[1], w_recv.at[1, k], (group, zm * 2 + y, core),
        )

    def side(s, k):
        if s == 1:
            ref, sem = wall.at[1, rows(k), half_cols], w_swap.at[0]
        else:
            v, part_rows = patch(k)
            ref, sem = far_wall.at[v, part_rows, half_lane], w_swap.at[1 + v]
        return remote(ref, ref, w_send.at[s + 1], sem, (cousin, dp, core))

    def swapped(ref, n):
        remote(ref, ref, w_send.at[2], w_swap.at[n], (cousin, dp, core)).wait_recv()

    def near_swapped():
        swapped(wall.at[1, :, rest_cols], 0)

    def far_swapped(v):
        swapped(far_wall.at[v, :, rest_lane], 1 + v)

    def relay_on(k):
        to_relay(k).wait_recv()
        mid_relay(k).start()

    def side_on(s, k):
        (mid_own(k) if s == 1 else mid_relay(k)).wait_recv()
        side(s, k).start()

    def own_copy():
        return pltpu.make_async_copy(w_ref, wall.at[0], own_sem.at[0])

    @pl.when(inner)
    def _():
        loop(0, chunks, lambda k: mid_own(k).start())

    @pl.when(outer)
    def _():
        to_relay(0).start()

    own_copy().start()

    length = len_ref[dp]
    position = lax.broadcasted_iota(jnp.int32, (tokens, cached), 1)
    bias[:, :cached] = jnp.where(position < length, 0.0, MASKED)
    bias[:, cached:] = jnp.where(
        lax.broadcasted_iota(jnp.int32, (tokens, tokens), 1)
        <= lax.broadcasted_iota(jnp.int32, (tokens, tokens), 0),
        0.0, MASKED,
    )
    for copy in loads:
        copy.wait()
    for j in range(table_ref.shape[1]):
        page = table_ref[0, j]
        keys[j * PAGE_TOKENS:(j + 1) * PAGE_TOKENS, :] = kp_ref[page]
        values[j * PAGE_TOKENS:(j + 1) * PAGE_TOKENS, :] = vp_ref[page]

    def act_at(slot, i):
        return act.at[slot, :, pl.ds(pl.multiple_of(i * step_cols, step_cols), step_cols)]

    def act_y(i):
        return remote(act_at(0, i), act_at(1, i), act_send.at[0], act_recv.at[1, i],
                      (group, peer, core))

    def act_z(i):
        return remote(act_at(0, i), act_at(2, i), act_send.at[1], act_recv.at[0, i],
                      (group, zp * 2 + y, core))

    def on_y(i):
        return remote(act_at(2, i), act_at(3, i), act_send.at[2], act_recv.at[1, steps],
                      (group, peer, core))

    def on_z(i):
        return remote(act_at(1, i), act_at(3, i), act_send.at[3], act_recv.at[1, steps],
                      (group, zp * 2 + y, core))

    over_y = steps - jnp.where(inner, near, far)
    over_z = steps - jnp.where(inner, far, near)

    def from_y(i):
        act_y(i).wait_recv()

        @pl.when(i < over_z)
        def _():
            on_z(i).start()

    def from_z(i):
        act_z(i).wait_recv()

        @pl.when(i >= over_y)
        def _():
            on_y(i).start()

    P = functools.partial

    def own_y(i):
        act_y(i).start()

    def attention_step(i):
        kv = (i * heads_per_step) // QUERY_GROUP
        kv_cols = pl.ds(pl.multiple_of(kv * HEAD_SIZE, HEAD_SIZE), HEAD_SIZE)
        for n in range(heads_per_step):
            start = pl.multiple_of((i * heads_per_step + n) * HEAD_SIZE, HEAD_SIZE)
            q = q_ref[:, pl.ds(start, HEAD_SIZE)]
            scores = lax.dot_general(
                q, keys[:, kv_cols], (((1,), (1,)), ((), ())), preferred_element_type=jnp.float32
            )
            scores = scores * SCALE + bias[...]
            weights = jnp.exp2(scores - jnp.max(scores, axis=-1, keepdims=True))
            total = jnp.sum(weights, axis=-1, keepdims=True)
            weighted = jnp.dot(
                weights.astype(jnp.bfloat16), values[:, kv_cols], preferred_element_type=jnp.float32
            )
            act[0, :, pl.ds(start, HEAD_SIZE)] = (weighted / total).astype(jnp.bfloat16)
        act_z(i).start()

        @pl.when(jnp.logical_or(outer, i < 2))
        def _():
            act_y(i).start()

        @pl.when(jnp.logical_and(outer, jnp.logical_and(i % 2 == 1, i < 2 * deep - 2)))
        def _():
            to_relay((i + 1) // 2).start()

        def at(n, *todo):
            @pl.when(jnp.logical_and(inner, i == n))
            def _():
                for act_now in todo:
                    act_now()

        at(3, P(side_on, 1, 0), P(relay_on, 0))
        at(4, P(from_z, 0), P(own_y, 2))
        at(5, P(side_on, 1, 1), P(from_y, 0))
        at(7, P(side_on, 1, 2), P(from_z, 1), P(own_y, 3))

    loop(0, steps, attention_step)

    @pl.when(outer)
    def _():
        for k in range(deep, pieces):
            to_relay(k).start()

    def shard_z(s):
        return jnp.where(s == 0, z, zm)

    def task(s, slot):
        return s * 4 + slot

    def swap(t):
        return remote(px_out.at[t], px_in.at[t], px_send.at[0], px_recv.at[t], (group, dp, other))

    my_rows = pl.ds(pl.multiple_of(core * rows_mine, rows_mine), rows_mine)
    mate_rows = pl.ds(pl.multiple_of(other * rows_mine, rows_mine), rows_mine)

    def place(s):
        zs = shard_z(s)
        to = zs // 2
        column = (zs * 2 + y - to * line) * cols
        return to, out_ref.at[my_rows, pl.ds(pl.multiple_of(column, 128), cols)]

    def owner(slot):
        return jnp.where(slot >= 2, zp, z) * 2 + jnp.where(slot % 2 == 1, 1 - y, y)

    def stays(s, slot):
        return jnp.logical_and(slot == 0, shard_z(s) // 2 == core)

    def begin(s, slot):
        t = task(s, slot)
        keep[t] = jnp.dot(act[slot], wall[s], preferred_element_type=jnp.float32)
        px_out[t] = keep[t, mate_rows, :].astype(jnp.bfloat16)
        swap(t).start()

    def finish(s, slot):
        t = task(s, slot)
        swap(t).wait_recv()
        stage[t] = (keep[t, my_rows, :] + px_in[t].astype(jnp.float32)).astype(jnp.bfloat16)
        to, ref = place(s)

        @pl.when(stays(s, slot))
        def _():
            pltpu.make_async_copy(stage.at[t], ref, out_recv.at[0]).start()

        @pl.when(jnp.logical_not(stays(s, slot)))
        def _():
            remote(stage.at[t], ref, out_send.at[0], out_recv.at[0], (group, owner(slot), to)).start()

    def far_swap(v, p):
        pair = pl.ds(p * 2, 2)
        return remote(far_out.at[v, pair], far_in.at[v, pair], px_send.at[1], far_recv.at[v, p],
                      (group, dp, other))

    def far_begin(v, p):
        pair = pl.ds(p * 2, 2)
        far_keep[v, pair] = jnp.dot(
            act[pair].reshape(2 * tokens, wide), far_wall[v], preferred_element_type=jnp.float32,
        ).reshape(2, tokens, unit)
        far_out[v, pair] = far_keep[v, pair, mate_rows, :].astype(jnp.bfloat16)
        far_swap(v, p).start()

    def far_stays(slot):
        return jnp.logical_and(slot == 0, 1 - half == core)

    def far_finish(v, p):
        far_swap(v, p).wait_recv()
        pair = pl.ds(p * 2, 2)
        far_stage[v, pair] = (
            far_keep[v, pair, my_rows, :] + far_in[v, pair].astype(jnp.float32)
        ).astype(jnp.bfloat16)
        zs = (line - 1) * (1 - half)
        to = zs // 2
        for n in (1, 0):
            slot = p * 2 + n
            for u in range(2):
                column = (zs * 2 + y - to * line) * cols + u * unit + v * lane
                ref = out_ref.at[my_rows, pl.ds(pl.multiple_of(column, 128), lane)]
                src = far_stage.at[v, slot, :, u * lane:(u + 1) * lane]
                if n:
                    remote(src, ref, out_send.at[1], out_recv.at[0], (group, owner(slot), to)).start()
                else:
                    @pl.when(far_stays(slot))
                    def _():
                        pltpu.make_async_copy(src, ref, out_recv.at[0]).start()

                    @pl.when(jnp.logical_not(far_stays(slot)))
                    def _():
                        remote(src, ref, out_send.at[1], out_recv.at[0], (group, owner(slot), to)).start()

    own_copy().wait()

    def run(count, kinds, duties, prompt):
        def each(n, what):
            for holds, which, acts in kinds:
                @pl.when(holds(n))
                def _():
                    acts[what](*which(n))

        def one(n):
            early = functools.reduce(jnp.logical_or, [n == m + 1 for m in prompt])

            for at, todo in duties.items():
                @pl.when(n == at)
                def _():
                    for act_now in todo:
                        act_now()

            @pl.when(n < count)
            def _():
                each(n, 0)

            @pl.when(jnp.logical_and(n > 0, jnp.logical_not(early)))
            def _():
                each(n - 1, 1)

        loop(0, count + 1, one)

    def corner_landed():
        remote(act.at[2], act.at[3], act_send.at[2], act_recv.at[1, steps], (group, peer, core)).wait_recv()

    near_tasks = (begin, finish)
    far_tasks = (far_begin, far_finish)

    @pl.when(outer)
    def _():
        run(4, [(lambda n: n >= 0, lambda n: (0, n), near_tasks)], {
            1: [P(finish, 0, 0), lambda: loop(0, steps, from_z), lambda: loop(0, steps, from_y)],
            3: [P(finish, 0, 2), corner_landed],
        }, (0, 2))

    @pl.when(inner)
    def _():
        def is_far(n):
            return jnp.logical_or(n >= 9, n == 6)

        def near_which(n):
            m = jnp.where(n < 7, n, n - 1)
            group = m // 2
            return m % 2, jnp.where(group == 0, 0, jnp.where(group == 3, 1, group + 1))

        def far_which(n):
            return n // 10, jnp.where(n % 4 == 2, 1, 0)

        kinds = [(lambda n: jnp.logical_not(is_far(n)), near_which, near_tasks), (is_far, far_which, far_tasks)]
        run(12, kinds, {
            0: [P(side_on, 1, 3), P(relay_on, 1), P(from_y, 1)],
            1: [P(side_on, 1, 4), P(from_z, 2), P(from_y, 2), P(finish, 0, 0), P(side_on, 1, 5), P(from_z, 3), P(own_y, 4),
                P(side_on, 1, 6), P(relay_on, 2), P(side_on, 1, 7), P(from_z, 4), P(from_z, 5), P(own_y, 5),
                P(side_on, 2, 0), P(relay_on, 3), P(side_on, 2, 1), near_swapped],
            2: [P(from_z, 6), P(side_on, 2, 2), P(from_z, 7), P(own_y, 6), P(own_y, 7)],
            3: [P(relay_on, 4), P(side_on, 2, 3)],
            4: [P(relay_on, 5), P(relay_on, 6), P(finish, 1, 2), P(side_on, 2, 4), P(relay_on, 7), P(side_on, 2, 5),
                P(relay_on, 8), corner_landed],
            5: [P(side_on, 2, 6), P(relay_on, 9)],
            6: [P(side_on, 2, 7), P(relay_on, 10), P(far_swapped, 0)],
            7: [P(side_on, 2, 8), P(relay_on, 11), lambda: loop(3, steps, from_y)],
            8: [P(side_on, 2, 9), P(side_on, 2, 10)],
            9: [P(side_on, 2, 11)],
            10: [P(far_finish, 0, 0), P(far_swapped, 1)],
        }, (0, 3, 9))

    def sent(ref, sem):
        remote(ref, ref, sem, sem, (group, dp, other)).wait_send()

    def sent_if(holds, ref, sem):
        @pl.when(holds)
        def _():
            sent(ref, sem)

    sent(act.at[0], act_send.at[0])
    sent(act.at[0], act_send.at[1])
    unit_ref = wall.at[0, :, 0:unit]
    sent(unit_ref, w_send.at[0])
    far_goes = jnp.logical_and(inner, core == half)
    far_mate = jnp.logical_and(inner, core != half)
    sent_if(inner, stage.at[0:7], out_send.at[0])
    sent_if(jnp.logical_and(outer, core == half), stage.at[0:3], out_send.at[0])
    sent_if(jnp.logical_and(outer, core != half), stage.at[0:4], out_send.at[0])
    sent_if(inner, px_out, px_send.at[0])
    sent_if(outer, px_out.at[0:4], px_send.at[0])
    sent_if(inner, far_out, px_send.at[1])
    sent_if(far_goes, far_stage, out_send.at[1])
    sent_if(far_mate, far_stage.at[:, 0:3], out_send.at[1])
    for n in range(1, 4):
        sent_if(inner, unit_ref, w_send.at[n])

    def columns(low, high):
        return act.at[0, :, low * step_cols:high * step_cols]

    for holds, y_count, z_count in ((inner, near, steps - far), (outer, far, steps - near)):
        if y_count:
            sent_if(holds, columns(0, y_count), act_send.at[2])
        if z_count:
            sent_if(holds, columns(0, z_count), act_send.at[3])

    remote(out_ref, out_ref, out_recv.at[0], out_recv.at[0], (group, dp, other)).wait_recv()


def square_program(line, queries, fresh_keys, fresh_values, key_pages, value_pages, table, lengths, weight):
    tokens, wide = queries.shape
    part, cols = weight.shape
    chunks = part // CHUNK
    steps = wide // 256
    unit = cols // 2
    span = table.shape[1] * PAGE_TOKENS + tokens
    kv_width = fresh_keys.shape[1]
    hbm = pl.BlockSpec(memory_space=pl.ANY)
    smem = pl.BlockSpec(memory_space=pltpu.SMEM)
    dma = pltpu.SemaphoreType.DMA
    bf16, f32 = jnp.bfloat16, jnp.float32
    heads = wide // HEAD_SIZE
    flops = 4 * heads * tokens * span * HEAD_SIZE + 2 * 24 * tokens * part * unit
    return pl.pallas_call(
        functools.partial(square_kernel, line),
        out_shape=jax.ShapeDtypeStruct((tokens, line * cols), bf16),
        in_specs=[hbm, hbm, hbm, hbm, hbm, smem, smem, hbm],
        out_specs=hbm,
        scratch_shapes=[
            pltpu.VMEM(queries.shape, bf16),
            pltpu.VMEM(key_pages.shape, bf16),
            pltpu.VMEM(value_pages.shape, bf16),
            pltpu.VMEM((4, tokens, wide), bf16),
            pltpu.VMEM((2, part, cols), bf16),
            pltpu.VMEM((2, part, unit), bf16),
            pltpu.VMEM((2, part, unit // 2), bf16),
            pltpu.VMEM((8, tokens // 2, cols), bf16),
            pltpu.VMEM((8, tokens // 2, cols), bf16),
            pltpu.VMEM((8, tokens, cols), f32),
            pltpu.VMEM((8, tokens // 2, cols), bf16),
            pltpu.VMEM((span, kv_width), bf16),
            pltpu.VMEM((span, kv_width), bf16),
            pltpu.VMEM((tokens, span), f32),
            dma((2, chunks + chunks // 2)),
            dma((3,)),
            dma((4,)),
            dma((chunks + chunks // 2,)),
            dma((1,)),
            dma((2, steps + 1)),
            dma((4,)),
            dma((8,)),
            dma((2,)),
            dma((1,)),
            dma((2,)),
            dma((5,)),
            pltpu.VMEM((2, 4, tokens // 2, unit), bf16),
            pltpu.VMEM((2, 4, tokens // 2, unit), bf16),
            pltpu.VMEM((2, 4, tokens, unit), f32),
            pltpu.VMEM((2, 4, tokens // 2, unit), bf16),
            dma((2, 2)),
        ],
        compiler_params=pltpu.CompilerParams(
            collective_id=0, has_side_effects=True, vmem_limit_bytes=60 * 1024 * 1024
        ),
        cost_estimate=pl.CostEstimate(
            flops=flops, bytes_accessed=8 * 1024 * 1024, transcendentals=heads * tokens * span
        ),
    )(queries, fresh_keys, fresh_values, key_pages, value_pages, table, lengths, weight)


def program_of(line):
    return square_program if line == 4 else shards_program


def solution(mesh):
    return jax.shard_map(
        functools.partial(program_of(mesh.shape["dp"] // 2), mesh.shape["dp"] // 2),
        mesh=mesh,
        in_specs=(
            P(("groups", "dp"), "tensor"),
            P(("groups", "dp"), "tensor"),
            P(("groups", "dp"), "tensor"),
            P(("groups", "dp"), None, "tensor"),
            P(("groups", "dp"), None, "tensor"),
            P(("groups", "dp"), None),
            P("groups"),
            P("tensor", "dp"),
        ),
        out_specs=P(("groups", "dp"), "tensor"),
        check_vma=False,
    )
```

```python
import functools

import jax
import jax.numpy as jnp
from jax import lax
from jax.experimental import pallas as pl
from jax.experimental.pallas import tpu as pltpu
from jax.sharding import PartitionSpec as P

HEAD_SIZE = 128
QUERY_GROUP = 8
PAGE_TOKENS = 128
CHUNK = 256
OUTER_ZY = 8
INNER_ZY = 5
SCALE = HEAD_SIZE ** (-0.5) * 1.4426950408889634
MASKED = -1e30


def kernel(
    line, q_ref, fk_ref, fv_ref, kp_ref, vp_ref, table_ref, len_ref, w_ref, out_ref,
    wbuf, act, stage, keys, values, bias,
    w_recv, w_next, w_side, own_send, act_recv, act_send, act_fwd, out_send, out_recv,
):
    group, dp, core = lax.axis_index("groups"), lax.axis_index("dp"), lax.axis_index("tensor")
    z, y = dp // 2, dp % 2
    half = group % 2
    cousin = group + 1 - 2 * half
    other = 1 - core
    peer = z * 2 + 1 - y
    shards = line // 2
    part, cols = w_ref.shape
    tokens = q_ref.shape[0]
    per_core = part // CHUNK
    per_half = per_core // 2
    own_core = z // shards
    own_slot = z - own_core * shards
    wide = act.shape[2] // 2
    step_cols = wide // per_core
    heads_per_step = step_cols // HEAD_SIZE
    heads_per_kv = QUERY_GROUP
    tile = min(cols, 256)
    tiles = cols // tile

    def remote(src, dst, send, recv, where):
        return pltpu.make_async_remote_copy(
            src_ref=src, dst_ref=dst, send_sem=send, recv_sem=recv,
            device_id=where, device_id_type=pl.DeviceIdType.MESH,
        )

    def rows(k):
        return pl.ds(pl.multiple_of(k * CHUNK, CHUNK), CHUNK)

    barrier = pltpu.get_barrier_semaphore()

    def greet(where):
        pl.semaphore_signal(barrier, inc=1, device_id=where, device_id_type=pl.DeviceIdType.MESH)

    greet((group, dp, other))
    greet((cousin, dp, core))
    greet((group, peer, core))

    @pl.when(z > 0)
    def _():
        greet((group, dp - 2, core))
        greet((group, dp - 2, other))

    @pl.when(z < line - 1)
    def _():
        greet((group, dp + 2, core))
        greet((group, dp + 2, other))

    neighbours = jnp.where(z > 0, 2, 0) + jnp.where(z < line - 1, 2, 0)
    pl.semaphore_wait(barrier, 3 + neighbours)

    def own_copy(k, side):
        slab = core * per_core + k
        where = (group, dp + 2 * side, own_core) if side else (group, dp, other)
        return remote(
            w_ref.at[rows(k)], wbuf.at[own_slot, rows(slab)],
            own_send.at[side + 1, k], w_recv.at[own_slot, slab], where,
        )

    def own_local(k):
        slab = core * per_core + k
        return pltpu.make_async_copy(
            w_ref.at[rows(k)], wbuf.at[own_slot, rows(slab)], w_recv.at[own_slot, slab]
        )

    def each_own(act_on):
        def one(j, carry):
            k = half * per_half + j

            @pl.when(z > 0)
            def _():
                act_on(own_copy(k, -1))

            @pl.when(z < line - 1)
            def _():
                act_on(own_copy(k, 1))

            return carry

        lax.fori_loop(0, per_half, one, 0)

        @pl.when(core != own_core)
        def _():
            lax.fori_loop(0, per_core, lambda k, carry: (act_on(own_copy(k, 0)), carry)[1], 0)

    each_own(lambda copy: copy.start())

    @pl.when(core == own_core)
    def _():
        lax.fori_loop(0, per_core, lambda k, carry: (own_local(k).start(), carry)[1], 0)

    def slab_of(i, which):
        return (i % 2) * per_core + which * per_half + i // 2

    def landed(slot, slab):
        remote(
            wbuf.at[slot, rows(slab)], wbuf.at[slot, rows(slab)],
            w_next.at[slot, slab], w_recv.at[slot, slab], (group, dp, other),
        ).wait_recv()

    def next_copy(slot, slab, step):
        return remote(
            wbuf.at[slot, rows(slab)], wbuf.at[slot, rows(slab)],
            w_next.at[slot, slab], w_recv.at[slot, slab], (group, dp + 2 * step, core),
        )

    def side_copy(slot, slab):
        return remote(
            wbuf.at[slot, rows(slab)], wbuf.at[slot, rows(slab)],
            w_side.at[slot, slab], w_recv.at[slot, slab], (cousin, dp, core),
        )

    def pass_on(slot, origin, i):
        slab = slab_of(i, half)
        landed(slot, slab)

        @pl.when(jnp.logical_and(origin < z, z < line - 1))
        def _():
            next_copy(slot, slab, 1).start()

        @pl.when(jnp.logical_and(origin > z, z > 0))
        def _():
            next_copy(slot, slab, -1).start()

        side_copy(slot, slab).start()

    length = len_ref[dp]
    cached = table_ref.shape[1] * PAGE_TOKENS
    for j in range(table_ref.shape[1]):
        page = table_ref[0, j]
        keys[j * PAGE_TOKENS:(j + 1) * PAGE_TOKENS, :] = kp_ref[page]
        values[j * PAGE_TOKENS:(j + 1) * PAGE_TOKENS, :] = vp_ref[page]
    keys[cached:, :] = fk_ref[...]
    values[cached:, :] = fv_ref[...]
    position = lax.broadcasted_iota(jnp.int32, (tokens, cached), 1)
    bias[:, :cached] = jnp.where(position < length, 0.0, MASKED)
    bias[:, cached:] = jnp.where(
        lax.broadcasted_iota(jnp.int32, (tokens, tokens), 1)
        <= lax.broadcasted_iota(jnp.int32, (tokens, tokens), 0),
        0.0, MASKED,
    )

    def act_cols(slab):
        return pl.ds(pl.multiple_of(slab * step_cols, step_cols), step_cols)

    def act_copy(i, to_peer):
        slab = core * per_core + i
        src = act.at[0, :, act_cols(slab)]
        if to_peer:
            return remote(src, act.at[1, :, act_cols(slab)], act_send.at[1, i],
                          act_recv.at[1, slab], (group, peer, core))
        return remote(src, src, act_send.at[0, i], act_recv.at[0, slab], (group, dp, other))

    def act_forward(i):
        slab = core * per_core + i
        ref = act.at[1, :, act_cols(slab)]
        return remote(ref, ref, act_fwd.at[i], act_recv.at[1, slab], (group, dp, other))

    def act_landed(block, slab):
        ref = act.at[block, :, act_cols(slab)]
        remote(ref, ref, act_fwd.at[0], act_recv.at[block, slab], (group, dp, other)).wait_recv()

    def relay(i):
        act_landed(1, core * per_core + i)
        act_forward(i).start()

    lag = 2

    def attention_step(i, carry):
        kv = (i * heads_per_step) // heads_per_kv
        kv_cols = pl.ds(pl.multiple_of(kv * HEAD_SIZE, HEAD_SIZE), HEAD_SIZE)
        for n in range(heads_per_step):
            head = i * heads_per_step + n
            q = q_ref[:, pl.ds(pl.multiple_of(head * HEAD_SIZE, HEAD_SIZE), HEAD_SIZE)]
            scores = lax.dot_general(
                q, keys[:, kv_cols], (((1,), (1,)), ((), ())), preferred_element_type=jnp.float32
            )
            scores = scores * SCALE + bias[...]
            weights = jnp.exp2(scores - jnp.max(scores, axis=-1, keepdims=True))
            total = jnp.sum(weights, axis=-1, keepdims=True)
            weighted = jnp.dot(
                weights.astype(jnp.bfloat16), values[:, kv_cols], preferred_element_type=jnp.float32
            )
            start = core * wide + head * HEAD_SIZE
            act[0, :, pl.ds(pl.multiple_of(start, HEAD_SIZE), HEAD_SIZE)] = (
                weighted / total
            ).astype(jnp.bfloat16)
        act_copy(i, True).start()
        act_copy(i, False).start()
        for side in (-1, 1):
            origin = z + side

            @pl.when(jnp.logical_and(
                jnp.logical_and(origin >= core * shards, origin < (core + 1) * shards), True))
            def _():
                pass_on(origin - core * shards, origin, i)

        @pl.when(i >= lag)
        def _():
            relay(i - lag)

        return carry

    lax.fori_loop(0, per_core, attention_step, 0)
    for i in range(per_core - lag, per_core):
        relay(i)

    def origin_of(p):
        low = core * shards
        inside = low + (z - low + p + shards * line) % shards
        return jnp.where(z < low, low + p, jnp.where(z >= low + shards, low + shards - 1 - p, inside))

    def out_cols(origin, n):
        start = (origin * 2 + y - core * 2 * shards) * cols + n * tile
        return pl.ds(pl.multiple_of(start, 128), tile)

    def out_copy(slot, n, column):
        return remote(
            stage.at[slot, n], out_ref.at[:, column], out_send.at[slot, n],
            out_recv.at[slot, n], (group, peer, core),
        )

    def product(block, slot, n):
        return jnp.dot(
            act[block], wbuf[slot, :, pl.ds(pl.multiple_of(n * tile, 128), tile)],
            preferred_element_type=jnp.float32,
        ).astype(jnp.bfloat16)

    def piece(origin, m):
        slot = origin - core * shards
        n = m % tiles
        column = out_cols(origin, n)

        @pl.when(m < tiles)
        def _():
            stage[slot, n] = product(1, slot, n)
            out_copy(slot, n, column).start()

        @pl.when(m >= tiles)
        def _():
            out_ref[:, column] = product(0, slot, n)

    def rest_landed(origin):
        slot = origin - core * shards

        def one(i, carry):
            landed(slot, slab_of(i, 1 - half))

            @pl.when(origin == z)
            def _():
                landed(slot, slab_of(i, half))

            return carry

        lax.fori_loop(0, per_core, one, 0)

    def acts_landed():
        def one(i, carry):
            act_landed(0, other * per_core + i)
            act_landed(1, other * per_core + i)
            return carry

        lax.fori_loop(0, per_core, one, 0)

    def shard_step(p, carry):
        origin = origin_of(p)
        before = origin_of(jnp.maximum(p - 1, 0))

        def chunk_step(i, inner):
            @pl.when(jnp.logical_or(origin > z + 1, origin < z - 1))
            def _():
                pass_on(origin - core * shards, origin, i)

            return inner

        lax.fori_loop(0, per_core, chunk_step, 0)

        @pl.when(p > 0)
        def _():
            @pl.when(p == 1)
            def _():
                acts_landed()

            rest_landed(before)
            lax.fori_loop(0, 2 * tiles, lambda m, inner: (piece(before, m), inner)[1], 0)

        return carry

    lax.fori_loop(0, shards, shard_step, 0)
    if shards == 1:
        acts_landed()
    last = origin_of(shards - 1)
    rest_landed(last)
    lax.fori_loop(0, 2 * tiles, lambda m, carry: (piece(last, m), carry)[1], 0)

    def finish(slot, carry):
        origin = core * shards + slot
        for n in range(tiles):
            start = (origin * 2 + 1 - y - core * 2 * shards) * cols + n * tile
            copy = out_copy(slot, n, pl.ds(pl.multiple_of(start, 128), tile))
            copy.wait_recv()
            copy.wait_send()

        @pl.when(origin != z)
        def _():
            def one(i, inner):
                slab = slab_of(i, half)

                @pl.when(jnp.logical_and(origin < z, z < line - 1))
                def _():
                    next_copy(slot, slab, 1).wait_send()

                @pl.when(jnp.logical_and(origin > z, z > 0))
                def _():
                    next_copy(slot, slab, -1).wait_send()

                side_copy(slot, slab).wait_send()
                return inner

            lax.fori_loop(0, per_core, one, 0)

        return carry

    lax.fori_loop(0, shards, finish, 0)

    def acts_sent(i, carry):
        act_copy(i, True).wait_send()
        act_copy(i, False).wait_send()
        act_forward(i).wait_send()
        return carry

    lax.fori_loop(0, per_core, acts_sent, 0)
    each_own(lambda copy: copy.wait_send())


def shards_program(line, queries, fresh_keys, fresh_values, key_pages, value_pages, table, lengths, weight):
    tokens, wide = queries.shape
    part, cols = weight.shape
    per_core = part // CHUNK
    shards = line // 2
    tile = min(cols, 256)
    tiles = cols // tile
    span = table.shape[1] * PAGE_TOKENS + tokens
    kv_width = fresh_keys.shape[1]
    out_width = 2 * shards * cols
    vmem = pl.BlockSpec(memory_space=pltpu.VMEM)
    smem = pl.BlockSpec(memory_space=pltpu.SMEM)
    dma = pltpu.SemaphoreType.DMA
    heads = wide // HEAD_SIZE
    flops = 4 * heads * tokens * span * HEAD_SIZE + 2 * 2 * tokens * 2 * part * shards * cols
    return pl.pallas_call(
        functools.partial(kernel, line),
        out_shape=jax.ShapeDtypeStruct((tokens, out_width), jnp.bfloat16),
        in_specs=[vmem, vmem, vmem, vmem, vmem, smem, smem, pl.BlockSpec(memory_space=pl.ANY)],
        out_specs=vmem,
        scratch_shapes=[
            pltpu.VMEM((shards, 2 * part, cols), jnp.bfloat16),
            pltpu.VMEM((2, tokens, 2 * wide), jnp.bfloat16),
            pltpu.VMEM((shards, tiles, tokens, tile), jnp.bfloat16),
            pltpu.VMEM((span, kv_width), jnp.bfloat16),
            pltpu.VMEM((span, kv_width), jnp.bfloat16),
            pltpu.VMEM((tokens, span), jnp.float32),
            dma((shards, 2 * per_core)),
            dma((shards, 2 * per_core)),
            dma((shards, 2 * per_core)),
            dma((3, per_core)),
            dma((2, 2 * per_core)),
            dma((2, per_core)),
            dma((per_core,)),
            dma((shards, tiles)),
            dma((shards, tiles)),
        ],
        compiler_params=pltpu.CompilerParams(
            collective_id=0, has_side_effects=True, vmem_limit_bytes=60 * 1024 * 1024
        ),
        cost_estimate=pl.CostEstimate(
            flops=flops, bytes_accessed=8 * 1024 * 1024, transcendentals=heads * tokens * span
        ),
    )(queries, fresh_keys, fresh_values, key_pages, value_pages, table, lengths, weight)


def square_kernel(
    line, q_hbm, fk_hbm, fv_hbm, kp_hbm, vp_hbm, table_ref, len_ref, w_ref, out_ref,
    q_ref, kp_ref, vp_ref, act, wall, far_wall, relay, px_out, px_in, keep, stage, keys, values, bias,
    w_recv, w_swap, w_send, r_recv, own_sem, act_recv, act_send,
    px_recv, px_send, out_recv, out_send, in_sem,
    far_out, far_in, far_keep, far_stage, far_recv,
):
    group, dp, core = lax.axis_index("groups"), lax.axis_index("dp"), lax.axis_index("tensor")
    z, y = dp // 2, dp % 2
    x = group % 2
    cousin = group + 1 - 2 * x
    other = 1 - core
    half = z // 2
    inner = z % 2 != half
    outer = jnp.logical_not(inner)
    zp = z + 1 - 2 * (z % 2)
    zm = jnp.where(inner, line - 1 - z, z)
    peer = z * 2 + 1 - y
    part, cols = w_ref.shape
    tokens, wide = q_ref.shape
    chunks = part // CHUNK
    unit = cols // 2
    lane = unit // 2
    tall = 2 * CHUNK
    rows_mine = tokens // 2
    steps = wide // 256
    step_cols = wide // steps
    heads_per_step = step_cols // HEAD_SIZE
    near, far = steps * OUTER_ZY // 8, steps * INNER_ZY // 8

    def remote(src, dst, send, recv, where):
        return pltpu.make_async_remote_copy(
            src_ref=src, dst_ref=dst, send_sem=send, recv_sem=recv,
            device_id=where, device_id_type=pl.DeviceIdType.MESH,
        )

    def loop(low, high, act_on):
        lax.fori_loop(low, high, lambda k, carry: (act_on(k), carry)[1], 0)

    def rows(k):
        return pl.ds(pl.multiple_of(k * CHUNK, CHUNK), CHUNK)

    cached = table_ref.shape[1] * PAGE_TOKENS

    loads = [
        pltpu.make_async_copy(kp_hbm, kp_ref, in_sem.at[0]),
        pltpu.make_async_copy(vp_hbm, vp_ref, in_sem.at[1]),
        pltpu.make_async_copy(fk_hbm, keys.at[cached:], in_sem.at[2]),
        pltpu.make_async_copy(fv_hbm, values.at[cached:], in_sem.at[3]),
        pltpu.make_async_copy(q_hbm, q_ref, in_sem.at[4]),
    ]
    for copy in loads:
        copy.start()

    barrier = pltpu.get_barrier_semaphore()

    def greet(where):
        pl.semaphore_signal(barrier, inc=1, device_id=where, device_id_type=pl.DeviceIdType.MESH)

    greet((group, dp, other))
    for chip in (peer, zp * 2 + y):
        greet((group, chip, core))
        greet((group, chip, other))

    @pl.when(inner)
    def _():
        greet((cousin, dp, core))
        greet((group, zm * 2 + y, core))

    pl.semaphore_wait(barrier, 5 + jnp.where(inner, 2, 0))

    half_cols = pl.ds(pl.multiple_of(x * unit, 128), unit)
    half_lane = pl.ds(pl.multiple_of(x * lane, 128), lane)
    rest_cols = pl.ds(pl.multiple_of((1 - x) * unit, 128), unit)
    rest_lane = pl.ds(pl.multiple_of((1 - x) * lane, 128), lane)
    deep = chunks // 2
    pieces = deep + chunks

    def patch(k):
        if isinstance(k, jax.Array) or k < deep:
            return 0, pl.ds(pl.multiple_of(k * tall, tall), tall)
        return 1, pl.ds((k - deep) * CHUNK, CHUNK)

    def mid_own(k):
        return remote(
            w_ref.at[rows(k), half_cols], wall.at[1, rows(k), half_cols],
            w_send.at[0], w_recv.at[0, k], (group, zm * 2 + y, core),
        )

    def to_relay(k):
        v, part_rows = patch(k)
        column = pl.ds(pl.multiple_of(x * unit + v * lane, 128), lane)
        return remote(
            w_ref.at[part_rows, column], relay.at[v, part_rows],
            w_send.at[0], r_recv.at[k], (group, zp * 2 + y, core),
        )

    def mid_relay(k):
        v, part_rows = patch(k)
        return remote(
            relay.at[v, part_rows], far_wall.at[v, part_rows, half_lane],
            w_send.at[1], w_recv.at[1, k], (group, zm * 2 + y, core),
        )

    def slant(k):
        v, part_rows = patch(k)
        return remote(
            relay.at[v, part_rows], far_wall.at[v, part_rows, half_lane],
            w_send.at[3], w_swap.at[1 + v], (cousin, zm * 2 + y, core),
        )

    def side(s, k):
        if s == 1:
            ref, sem = wall.at[1, rows(k), half_cols], w_swap.at[0]
        else:
            v, part_rows = patch(k)
            ref, sem = far_wall.at[v, part_rows, half_lane], w_swap.at[1 + v]
        return remote(ref, ref, w_send.at[s + 1], sem, (cousin, dp, core))

    def swapped(ref, n):
        remote(ref, ref, w_send.at[2], w_swap.at[n], (cousin, dp, core)).wait_recv()

    def near_swapped():
        swapped(wall.at[1, :, rest_cols], 0)

    def far_swapped(v):
        swapped(far_wall.at[v, :, rest_lane], 1 + v)

    def relay_on(k):
        to_relay(k).wait_recv()
        mid_relay(k).start()

    def side_on(s, k):
        (mid_own(k) if s == 1 else mid_relay(k)).wait_recv()
        side(s, k).start()

    def own_copy():
        return pltpu.make_async_copy(w_ref, wall.at[0], own_sem.at[0])

    @pl.when(inner)
    def _():
        loop(0, chunks, lambda k: mid_own(k).start())

    @pl.when(outer)
    def _():
        to_relay(0).start()

    own_copy().start()

    length = len_ref[dp]
    position = lax.broadcasted_iota(jnp.int32, (tokens, cached), 1)
    bias[:, :cached] = jnp.where(position < length, 0.0, MASKED)
    bias[:, cached:] = jnp.where(
        lax.broadcasted_iota(jnp.int32, (tokens, tokens), 1)
        <= lax.broadcasted_iota(jnp.int32, (tokens, tokens), 0),
        0.0, MASKED,
    )
    for copy in loads:
        copy.wait()
    for j in range(table_ref.shape[1]):
        page = table_ref[0, j]
        keys[j * PAGE_TOKENS:(j + 1) * PAGE_TOKENS, :] = kp_ref[page]
        values[j * PAGE_TOKENS:(j + 1) * PAGE_TOKENS, :] = vp_ref[page]

    def act_at(slot, i):
        return act.at[slot, :, pl.ds(pl.multiple_of(i * step_cols, step_cols), step_cols)]

    def act_y(i):
        return remote(act_at(0, i), act_at(1, i), act_send.at[0], act_recv.at[1, i],
                      (group, peer, core))

    def act_z(i):
        return remote(act_at(0, i), act_at(2, i), act_send.at[1], act_recv.at[0, i],
                      (group, zp * 2 + y, core))

    def on_y(i):
        return remote(act_at(2, i), act_at(3, i), act_send.at[2], act_recv.at[1, steps],
                      (group, peer, core))

    def on_z(i):
        return remote(act_at(1, i), act_at(3, i), act_send.at[3], act_recv.at[1, steps],
                      (group, zp * 2 + y, core))

    over_y = steps - jnp.where(inner, near, far)
    over_z = steps - jnp.where(inner, far, near)

    def from_y(i):
        act_y(i).wait_recv()

        @pl.when(i < over_z)
        def _():
            on_z(i).start()

    def from_z(i):
        act_z(i).wait_recv()

        @pl.when(i >= over_y)
        def _():
            on_y(i).start()

    P = functools.partial

    def own_y(i):
        act_y(i).start()

    def attention_step(i):
        kv = (i * heads_per_step) // QUERY_GROUP
        kv_cols = pl.ds(pl.multiple_of(kv * HEAD_SIZE, HEAD_SIZE), HEAD_SIZE)
        for n in range(heads_per_step):
            start = pl.multiple_of((i * heads_per_step + n) * HEAD_SIZE, HEAD_SIZE)
            q = q_ref[:, pl.ds(start, HEAD_SIZE)]
            scores = lax.dot_general(
                q, keys[:, kv_cols], (((1,), (1,)), ((), ())), preferred_element_type=jnp.float32
            )
            scores = scores * SCALE + bias[...]
            weights = jnp.exp2(scores - jnp.max(scores, axis=-1, keepdims=True))
            total = jnp.sum(weights, axis=-1, keepdims=True)
            weighted = jnp.dot(
                weights.astype(jnp.bfloat16), values[:, kv_cols], preferred_element_type=jnp.float32
            )
            act[0, :, pl.ds(start, HEAD_SIZE)] = (weighted / total).astype(jnp.bfloat16)
        act_z(i).start()

        @pl.when(jnp.logical_or(outer, i < 2))
        def _():
            act_y(i).start()

        @pl.when(jnp.logical_and(outer, jnp.logical_and(i % 2 == 1, i < 2 * deep - 2)))
        def _():
            to_relay((i + 1) // 2).start()

        def at(n, *todo):
            @pl.when(jnp.logical_and(inner, i == n))
            def _():
                for act_now in todo:
                    act_now()

        at(3, P(side_on, 1, 0), P(relay_on, 0))
        at(4, P(from_z, 0), P(own_y, 2))
        at(5, P(side_on, 1, 1), P(from_y, 0))
        at(7, P(side_on, 1, 2), P(from_z, 1), P(own_y, 3))

    loop(0, steps, attention_step)

    @pl.when(outer)
    def _():
        for k in range(deep, pieces):
            to_relay(k).start()

    def shard_z(s):
        return jnp.where(s == 0, z, zm)

    def task(s, slot):
        return s * 4 + slot

    def swap(t):
        return remote(px_out.at[t], px_in.at[t], px_send.at[0], px_recv.at[t], (group, dp, other))

    my_rows = pl.ds(pl.multiple_of(core * rows_mine, rows_mine), rows_mine)
    mate_rows = pl.ds(pl.multiple_of(other * rows_mine, rows_mine), rows_mine)

    def place(s):
        zs = shard_z(s)
        to = zs // 2
        column = (zs * 2 + y - to * line) * cols
        return to, out_ref.at[my_rows, pl.ds(pl.multiple_of(column, 128), cols)]

    def owner(slot):
        return jnp.where(slot >= 2, zp, z) * 2 + jnp.where(slot % 2 == 1, 1 - y, y)

    def stays(s, slot):
        return jnp.logical_and(slot == 0, shard_z(s) // 2 == core)

    def begin(s, slot):
        t = task(s, slot)
        keep[t] = jnp.dot(act[slot], wall[s], preferred_element_type=jnp.float32)
        px_out[t] = keep[t, mate_rows, :].astype(jnp.bfloat16)
        swap(t).start()

    def finish(s, slot):
        t = task(s, slot)
        swap(t).wait_recv()
        stage[t] = (keep[t, my_rows, :] + px_in[t].astype(jnp.float32)).astype(jnp.bfloat16)
        to, ref = place(s)

        @pl.when(stays(s, slot))
        def _():
            pltpu.make_async_copy(stage.at[t], ref, out_recv.at[0]).start()

        @pl.when(jnp.logical_not(stays(s, slot)))
        def _():
            remote(stage.at[t], ref, out_send.at[0], out_recv.at[0], (group, owner(slot), to)).start()

    def far_swap(v, p):
        pair = pl.ds(p * 2, 2)
        return remote(far_out.at[v, pair], far_in.at[v, pair], px_send.at[1], far_recv.at[v, p],
                      (group, dp, other))

    def far_begin(v, p):
        pair = pl.ds(p * 2, 2)
        far_keep[v, pair] = jnp.dot(
            act[pair].reshape(2 * tokens, wide), far_wall[v], preferred_element_type=jnp.float32,
        ).reshape(2, tokens, unit)
        far_out[v, pair] = far_keep[v, pair, mate_rows, :].astype(jnp.bfloat16)
        far_swap(v, p).start()

    def far_stays(slot):
        return jnp.logical_and(slot == 0, 1 - half == core)

    def far_finish(v, p):
        far_swap(v, p).wait_recv()
        pair = pl.ds(p * 2, 2)
        far_stage[v, pair] = (
            far_keep[v, pair, my_rows, :] + far_in[v, pair].astype(jnp.float32)
        ).astype(jnp.bfloat16)
        zs = (line - 1) * (1 - half)
        to = zs // 2
        for n in (1, 0):
            slot = p * 2 + n
            for u in range(2):
                column = (zs * 2 + y - to * line) * cols + u * unit + v * lane
                ref = out_ref.at[my_rows, pl.ds(pl.multiple_of(column, 128), lane)]
                src = far_stage.at[v, slot, :, u * lane:(u + 1) * lane]
                if n:
                    remote(src, ref, out_send.at[1], out_recv.at[0], (group, owner(slot), to)).start()
                else:
                    @pl.when(far_stays(slot))
                    def _():
                        pltpu.make_async_copy(src, ref, out_recv.at[0]).start()

                    @pl.when(jnp.logical_not(far_stays(slot)))
                    def _():
                        remote(src, ref, out_send.at[1], out_recv.at[0], (group, owner(slot), to)).start()

    own_copy().wait()

    def run(count, kinds, duties, prompt):
        def each(n, what):
            for holds, which, acts in kinds:
                @pl.when(holds(n))
                def _():
                    acts[what](*which(n))

        def one(n):
            early = functools.reduce(jnp.logical_or, [n == m + 1 for m in prompt])

            for at, todo in duties.items():
                @pl.when(n == at)
                def _():
                    for act_now in todo:
                        act_now()

            @pl.when(n < count)
            def _():
                each(n, 0)

            @pl.when(jnp.logical_and(n > 0, jnp.logical_not(early)))
            def _():
                each(n - 1, 1)

        loop(0, count + 1, one)

    def corner_landed():
        remote(act.at[2], act.at[3], act_send.at[2], act_recv.at[1, steps], (group, peer, core)).wait_recv()

    near_tasks = (begin, finish)
    far_tasks = (far_begin, far_finish)

    @pl.when(outer)
    def _():
        run(4, [(lambda n: n >= 0, lambda n: (0, n), near_tasks)], {
            1: [P(finish, 0, 0), lambda: loop(0, steps, from_z), lambda: loop(0, steps, from_y)],
            3: [P(finish, 0, 2), corner_landed],
        }, (0, 2))

    @pl.when(inner)
    def _():
        def is_far(n):
            return jnp.logical_or(n >= 9, n == 6)

        def near_which(n):
            m = jnp.where(n < 7, n, n - 1)
            group = m // 2
            return m % 2, jnp.where(group == 0, 0, jnp.where(group == 3, 1, group + 1))

        def far_which(n):
            return n // 10, jnp.where(n % 4 == 2, 1, 0)

        last = pieces - 1
        kinds = [(lambda n: jnp.logical_not(is_far(n)), near_which, near_tasks), (is_far, far_which, far_tasks)]
        run(12, kinds, {
            0: [P(side_on, 1, 3), P(relay_on, 1), P(from_y, 1)],
            1: [P(side_on, 1, 4), P(from_z, 2), P(from_y, 2), P(finish, 0, 0), P(side_on, 1, 5), P(from_z, 3), P(own_y, 4),
                P(side_on, 1, 6), P(relay_on, 2), P(side_on, 1, 7), P(from_z, 4), P(from_z, 5), P(own_y, 5),
                P(side_on, 2, 0), P(relay_on, 3), P(side_on, 2, 1), near_swapped],
            2: [P(from_z, 6), P(side_on, 2, 2), P(from_z, 7), P(own_y, 6), P(own_y, 7)],
            3: [P(relay_on, 4), P(side_on, 2, 3)],
            4: [P(relay_on, 5), P(relay_on, 6), P(finish, 1, 2), P(side_on, 2, 4), P(relay_on, 7), P(side_on, 2, 5),
                P(relay_on, 8), corner_landed],
            5: [P(side_on, 2, 6), P(relay_on, 9)],
            6: [P(side_on, 2, 7), P(relay_on, 10), P(far_swapped, 0)],
            7: [P(side_on, 2, 8), P(relay_on, last), slant(last).start, P(side_on, 2, 9), lambda: loop(3, steps, from_y),
                P(side_on, 2, 10)],
            10: [P(far_finish, 0, 0), mid_relay(last).wait_recv, P(far_swapped, 1)],
        }, (0, 3, 9))

    def sent(ref, sem):
        remote(ref, ref, sem, sem, (group, dp, other)).wait_send()

    def sent_if(holds, ref, sem):
        @pl.when(holds)
        def _():
            sent(ref, sem)

    sent(act.at[0], act_send.at[0])
    sent(act.at[0], act_send.at[1])
    unit_ref = wall.at[0, :, 0:unit]
    sent(unit_ref, w_send.at[0])
    far_goes = jnp.logical_and(inner, core == half)
    far_mate = jnp.logical_and(inner, core != half)
    sent_if(inner, stage.at[0:7], out_send.at[0])
    sent_if(jnp.logical_and(outer, core == half), stage.at[0:3], out_send.at[0])
    sent_if(jnp.logical_and(outer, core != half), stage.at[0:4], out_send.at[0])
    sent_if(inner, px_out, px_send.at[0])
    sent_if(outer, px_out.at[0:4], px_send.at[0])
    sent_if(inner, far_out, px_send.at[1])
    sent_if(far_goes, far_stage, out_send.at[1])
    sent_if(far_mate, far_stage.at[:, 0:3], out_send.at[1])
    for n in range(1, 4):
        sent_if(inner, unit_ref, w_send.at[n])

    def columns(low, high):
        return act.at[0, :, low * step_cols:high * step_cols]

    for holds, y_count, z_count in ((inner, near, steps - far), (outer, far, steps - near)):
        if y_count:
            sent_if(holds, columns(0, y_count), act_send.at[2])
        if z_count:
            sent_if(holds, columns(0, z_count), act_send.at[3])

    remote(out_ref, out_ref, out_recv.at[0], out_recv.at[0], (group, dp, other)).wait_recv()


def square_program(line, queries, fresh_keys, fresh_values, key_pages, value_pages, table, lengths, weight):
    tokens, wide = queries.shape
    part, cols = weight.shape
    chunks = part // CHUNK
    steps = wide // 256
    unit = cols // 2
    span = table.shape[1] * PAGE_TOKENS + tokens
    kv_width = fresh_keys.shape[1]
    hbm = pl.BlockSpec(memory_space=pl.ANY)
    smem = pl.BlockSpec(memory_space=pltpu.SMEM)
    dma = pltpu.SemaphoreType.DMA
    bf16, f32 = jnp.bfloat16, jnp.float32
    heads = wide // HEAD_SIZE
    flops = 4 * heads * tokens * span * HEAD_SIZE + 2 * 24 * tokens * part * unit
    return pl.pallas_call(
        functools.partial(square_kernel, line),
        out_shape=jax.ShapeDtypeStruct((tokens, line * cols), bf16),
        in_specs=[hbm, hbm, hbm, hbm, hbm, smem, smem, hbm],
        out_specs=hbm,
        scratch_shapes=[
            pltpu.VMEM(queries.shape, bf16),
            pltpu.VMEM(key_pages.shape, bf16),
            pltpu.VMEM(value_pages.shape, bf16),
            pltpu.VMEM((4, tokens, wide), bf16),
            pltpu.VMEM((2, part, cols), bf16),
            pltpu.VMEM((2, part, unit), bf16),
            pltpu.VMEM((2, part, unit // 2), bf16),
            pltpu.VMEM((8, tokens // 2, cols), bf16),
            pltpu.VMEM((8, tokens // 2, cols), bf16),
            pltpu.VMEM((8, tokens, cols), f32),
            pltpu.VMEM((8, tokens // 2, cols), bf16),
            pltpu.VMEM((span, kv_width), bf16),
            pltpu.VMEM((span, kv_width), bf16),
            pltpu.VMEM((tokens, span), f32),
            dma((2, chunks + chunks // 2)),
            dma((3,)),
            dma((4,)),
            dma((chunks + chunks // 2,)),
            dma((1,)),
            dma((2, steps + 1)),
            dma((4,)),
            dma((8,)),
            dma((2,)),
            dma((1,)),
            dma((2,)),
            dma((5,)),
            pltpu.VMEM((2, 4, tokens // 2, unit), bf16),
            pltpu.VMEM((2, 4, tokens // 2, unit), bf16),
            pltpu.VMEM((2, 4, tokens, unit), f32),
            pltpu.VMEM((2, 4, tokens // 2, unit), bf16),
            dma((2, 2)),
        ],
        compiler_params=pltpu.CompilerParams(
            collective_id=0, has_side_effects=True, vmem_limit_bytes=60 * 1024 * 1024
        ),
        cost_estimate=pl.CostEstimate(
            flops=flops, bytes_accessed=8 * 1024 * 1024, transcendentals=heads * tokens * span
        ),
    )(queries, fresh_keys, fresh_values, key_pages, value_pages, table, lengths, weight)


def program_of(line):
    return square_program if line == 4 else shards_program


def solution(mesh):
    return jax.shard_map(
        functools.partial(program_of(mesh.shape["dp"] // 2), mesh.shape["dp"] // 2),
        mesh=mesh,
        in_specs=(
            P(("groups", "dp"), "tensor"),
            P(("groups", "dp"), "tensor"),
            P(("groups", "dp"), "tensor"),
            P(("groups", "dp"), None, "tensor"),
            P(("groups", "dp"), None, "tensor"),
            P(("groups", "dp"), None),
            P("groups"),
            P("tensor", "dp"),
        ),
        out_specs=P(("groups", "dp"), "tensor"),
        check_vma=False,
    )
```

```python
import functools

import jax
import jax.numpy as jnp
from jax import lax
from jax.experimental import pallas as pl
from jax.experimental.pallas import tpu as pltpu
from jax.sharding import PartitionSpec as P

HEAD_SIZE = 128
QUERY_GROUP = 8
PAGE_TOKENS = 128
CHUNK = 256
OUTER_ZY = 8
INNER_ZY = 5
SCALE = HEAD_SIZE ** (-0.5) * 1.4426950408889634
MASKED = -1e30


def kernel(
    line, q_ref, fk_ref, fv_ref, kp_ref, vp_ref, table_ref, len_ref, w_ref, out_ref,
    wbuf, act, stage, keys, values, bias,
    w_recv, w_next, w_side, own_send, act_recv, act_send, act_fwd, out_send, out_recv,
):
    group, dp, core = lax.axis_index("groups"), lax.axis_index("dp"), lax.axis_index("tensor")
    z, y = dp // 2, dp % 2
    half = group % 2
    cousin = group + 1 - 2 * half
    other = 1 - core
    peer = z * 2 + 1 - y
    shards = line // 2
    part, cols = w_ref.shape
    tokens = q_ref.shape[0]
    per_core = part // CHUNK
    per_half = per_core // 2
    own_core = z // shards
    own_slot = z - own_core * shards
    wide = act.shape[2] // 2
    step_cols = wide // per_core
    heads_per_step = step_cols // HEAD_SIZE
    heads_per_kv = QUERY_GROUP
    tile = min(cols, 256)
    tiles = cols // tile

    def remote(src, dst, send, recv, where):
        return pltpu.make_async_remote_copy(
            src_ref=src, dst_ref=dst, send_sem=send, recv_sem=recv,
            device_id=where, device_id_type=pl.DeviceIdType.MESH,
        )

    def rows(k):
        return pl.ds(pl.multiple_of(k * CHUNK, CHUNK), CHUNK)

    barrier = pltpu.get_barrier_semaphore()

    def greet(where):
        pl.semaphore_signal(barrier, inc=1, device_id=where, device_id_type=pl.DeviceIdType.MESH)

    greet((group, dp, other))
    greet((cousin, dp, core))
    greet((group, peer, core))

    @pl.when(z > 0)
    def _():
        greet((group, dp - 2, core))
        greet((group, dp - 2, other))

    @pl.when(z < line - 1)
    def _():
        greet((group, dp + 2, core))
        greet((group, dp + 2, other))

    neighbours = jnp.where(z > 0, 2, 0) + jnp.where(z < line - 1, 2, 0)
    pl.semaphore_wait(barrier, 3 + neighbours)

    def own_copy(k, side):
        slab = core * per_core + k
        where = (group, dp + 2 * side, own_core) if side else (group, dp, other)
        return remote(
            w_ref.at[rows(k)], wbuf.at[own_slot, rows(slab)],
            own_send.at[side + 1, k], w_recv.at[own_slot, slab], where,
        )

    def own_local(k):
        slab = core * per_core + k
        return pltpu.make_async_copy(
            w_ref.at[rows(k)], wbuf.at[own_slot, rows(slab)], w_recv.at[own_slot, slab]
        )

    def each_own(act_on):
        def one(j, carry):
            k = half * per_half + j

            @pl.when(z > 0)
            def _():
                act_on(own_copy(k, -1))

            @pl.when(z < line - 1)
            def _():
                act_on(own_copy(k, 1))

            return carry

        lax.fori_loop(0, per_half, one, 0)

        @pl.when(core != own_core)
        def _():
            lax.fori_loop(0, per_core, lambda k, carry: (act_on(own_copy(k, 0)), carry)[1], 0)

    each_own(lambda copy: copy.start())

    @pl.when(core == own_core)
    def _():
        lax.fori_loop(0, per_core, lambda k, carry: (own_local(k).start(), carry)[1], 0)

    def slab_of(i, which):
        return (i % 2) * per_core + which * per_half + i // 2

    def landed(slot, slab):
        remote(
            wbuf.at[slot, rows(slab)], wbuf.at[slot, rows(slab)],
            w_next.at[slot, slab], w_recv.at[slot, slab], (group, dp, other),
        ).wait_recv()

    def next_copy(slot, slab, step):
        return remote(
            wbuf.at[slot, rows(slab)], wbuf.at[slot, rows(slab)],
            w_next.at[slot, slab], w_recv.at[slot, slab], (group, dp + 2 * step, core),
        )

    def side_copy(slot, slab):
        return remote(
            wbuf.at[slot, rows(slab)], wbuf.at[slot, rows(slab)],
            w_side.at[slot, slab], w_recv.at[slot, slab], (cousin, dp, core),
        )

    def pass_on(slot, origin, i):
        slab = slab_of(i, half)
        landed(slot, slab)

        @pl.when(jnp.logical_and(origin < z, z < line - 1))
        def _():
            next_copy(slot, slab, 1).start()

        @pl.when(jnp.logical_and(origin > z, z > 0))
        def _():
            next_copy(slot, slab, -1).start()

        side_copy(slot, slab).start()

    length = len_ref[dp]
    cached = table_ref.shape[1] * PAGE_TOKENS
    for j in range(table_ref.shape[1]):
        page = table_ref[0, j]
        keys[j * PAGE_TOKENS:(j + 1) * PAGE_TOKENS, :] = kp_ref[page]
        values[j * PAGE_TOKENS:(j + 1) * PAGE_TOKENS, :] = vp_ref[page]
    keys[cached:, :] = fk_ref[...]
    values[cached:, :] = fv_ref[...]
    position = lax.broadcasted_iota(jnp.int32, (tokens, cached), 1)
    bias[:, :cached] = jnp.where(position < length, 0.0, MASKED)
    bias[:, cached:] = jnp.where(
        lax.broadcasted_iota(jnp.int32, (tokens, tokens), 1)
        <= lax.broadcasted_iota(jnp.int32, (tokens, tokens), 0),
        0.0, MASKED,
    )

    def act_cols(slab):
        return pl.ds(pl.multiple_of(slab * step_cols, step_cols), step_cols)

    def act_copy(i, to_peer):
        slab = core * per_core + i
        src = act.at[0, :, act_cols(slab)]
        if to_peer:
            return remote(src, act.at[1, :, act_cols(slab)], act_send.at[1, i],
                          act_recv.at[1, slab], (group, peer, core))
        return remote(src, src, act_send.at[0, i], act_recv.at[0, slab], (group, dp, other))

    def act_forward(i):
        slab = core * per_core + i
        ref = act.at[1, :, act_cols(slab)]
        return remote(ref, ref, act_fwd.at[i], act_recv.at[1, slab], (group, dp, other))

    def act_landed(block, slab):
        ref = act.at[block, :, act_cols(slab)]
        remote(ref, ref, act_fwd.at[0], act_recv.at[block, slab], (group, dp, other)).wait_recv()

    def relay(i):
        act_landed(1, core * per_core + i)
        act_forward(i).start()

    lag = 2

    def attention_step(i, carry):
        kv = (i * heads_per_step) // heads_per_kv
        kv_cols = pl.ds(pl.multiple_of(kv * HEAD_SIZE, HEAD_SIZE), HEAD_SIZE)
        for n in range(heads_per_step):
            head = i * heads_per_step + n
            q = q_ref[:, pl.ds(pl.multiple_of(head * HEAD_SIZE, HEAD_SIZE), HEAD_SIZE)]
            scores = lax.dot_general(
                q, keys[:, kv_cols], (((1,), (1,)), ((), ())), preferred_element_type=jnp.float32
            )
            scores = scores * SCALE + bias[...]
            weights = jnp.exp2(scores - jnp.max(scores, axis=-1, keepdims=True))
            total = jnp.sum(weights, axis=-1, keepdims=True)
            weighted = jnp.dot(
                weights.astype(jnp.bfloat16), values[:, kv_cols], preferred_element_type=jnp.float32
            )
            start = core * wide + head * HEAD_SIZE
            act[0, :, pl.ds(pl.multiple_of(start, HEAD_SIZE), HEAD_SIZE)] = (
                weighted / total
            ).astype(jnp.bfloat16)
        act_copy(i, True).start()
        act_copy(i, False).start()
        for side in (-1, 1):
            origin = z + side

            @pl.when(jnp.logical_and(
                jnp.logical_and(origin >= core * shards, origin < (core + 1) * shards), True))
            def _():
                pass_on(origin - core * shards, origin, i)

        @pl.when(i >= lag)
        def _():
            relay(i - lag)

        return carry

    lax.fori_loop(0, per_core, attention_step, 0)
    for i in range(per_core - lag, per_core):
        relay(i)

    def origin_of(p):
        low = core * shards
        inside = low + (z - low + p + shards * line) % shards
        return jnp.where(z < low, low + p, jnp.where(z >= low + shards, low + shards - 1 - p, inside))

    def out_cols(origin, n):
        start = (origin * 2 + y - core * 2 * shards) * cols + n * tile
        return pl.ds(pl.multiple_of(start, 128), tile)

    def out_copy(slot, n, column):
        return remote(
            stage.at[slot, n], out_ref.at[:, column], out_send.at[slot, n],
            out_recv.at[slot, n], (group, peer, core),
        )

    def product(block, slot, n):
        return jnp.dot(
            act[block], wbuf[slot, :, pl.ds(pl.multiple_of(n * tile, 128), tile)],
            preferred_element_type=jnp.float32,
        ).astype(jnp.bfloat16)

    def piece(origin, m):
        slot = origin - core * shards
        n = m % tiles
        column = out_cols(origin, n)

        @pl.when(m < tiles)
        def _():
            stage[slot, n] = product(1, slot, n)
            out_copy(slot, n, column).start()

        @pl.when(m >= tiles)
        def _():
            out_ref[:, column] = product(0, slot, n)

    def rest_landed(origin):
        slot = origin - core * shards

        def one(i, carry):
            landed(slot, slab_of(i, 1 - half))

            @pl.when(origin == z)
            def _():
                landed(slot, slab_of(i, half))

            return carry

        lax.fori_loop(0, per_core, one, 0)

    def acts_landed():
        def one(i, carry):
            act_landed(0, other * per_core + i)
            act_landed(1, other * per_core + i)
            return carry

        lax.fori_loop(0, per_core, one, 0)

    def shard_step(p, carry):
        origin = origin_of(p)
        before = origin_of(jnp.maximum(p - 1, 0))

        def chunk_step(i, inner):
            @pl.when(jnp.logical_or(origin > z + 1, origin < z - 1))
            def _():
                pass_on(origin - core * shards, origin, i)

            return inner

        lax.fori_loop(0, per_core, chunk_step, 0)

        @pl.when(p > 0)
        def _():
            @pl.when(p == 1)
            def _():
                acts_landed()

            rest_landed(before)
            lax.fori_loop(0, 2 * tiles, lambda m, inner: (piece(before, m), inner)[1], 0)

        return carry

    lax.fori_loop(0, shards, shard_step, 0)
    if shards == 1:
        acts_landed()
    last = origin_of(shards - 1)
    rest_landed(last)
    lax.fori_loop(0, 2 * tiles, lambda m, carry: (piece(last, m), carry)[1], 0)

    def finish(slot, carry):
        origin = core * shards + slot
        for n in range(tiles):
            start = (origin * 2 + 1 - y - core * 2 * shards) * cols + n * tile
            copy = out_copy(slot, n, pl.ds(pl.multiple_of(start, 128), tile))
            copy.wait_recv()
            copy.wait_send()

        @pl.when(origin != z)
        def _():
            def one(i, inner):
                slab = slab_of(i, half)

                @pl.when(jnp.logical_and(origin < z, z < line - 1))
                def _():
                    next_copy(slot, slab, 1).wait_send()

                @pl.when(jnp.logical_and(origin > z, z > 0))
                def _():
                    next_copy(slot, slab, -1).wait_send()

                side_copy(slot, slab).wait_send()
                return inner

            lax.fori_loop(0, per_core, one, 0)

        return carry

    lax.fori_loop(0, shards, finish, 0)

    def acts_sent(i, carry):
        act_copy(i, True).wait_send()
        act_copy(i, False).wait_send()
        act_forward(i).wait_send()
        return carry

    lax.fori_loop(0, per_core, acts_sent, 0)
    each_own(lambda copy: copy.wait_send())


def shards_program(line, queries, fresh_keys, fresh_values, key_pages, value_pages, table, lengths, weight):
    tokens, wide = queries.shape
    part, cols = weight.shape
    per_core = part // CHUNK
    shards = line // 2
    tile = min(cols, 256)
    tiles = cols // tile
    span = table.shape[1] * PAGE_TOKENS + tokens
    kv_width = fresh_keys.shape[1]
    out_width = 2 * shards * cols
    vmem = pl.BlockSpec(memory_space=pltpu.VMEM)
    smem = pl.BlockSpec(memory_space=pltpu.SMEM)
    dma = pltpu.SemaphoreType.DMA
    heads = wide // HEAD_SIZE
    flops = 4 * heads * tokens * span * HEAD_SIZE + 2 * 2 * tokens * 2 * part * shards * cols
    return pl.pallas_call(
        functools.partial(kernel, line),
        out_shape=jax.ShapeDtypeStruct((tokens, out_width), jnp.bfloat16),
        in_specs=[vmem, vmem, vmem, vmem, vmem, smem, smem, pl.BlockSpec(memory_space=pl.ANY)],
        out_specs=vmem,
        scratch_shapes=[
            pltpu.VMEM((shards, 2 * part, cols), jnp.bfloat16),
            pltpu.VMEM((2, tokens, 2 * wide), jnp.bfloat16),
            pltpu.VMEM((shards, tiles, tokens, tile), jnp.bfloat16),
            pltpu.VMEM((span, kv_width), jnp.bfloat16),
            pltpu.VMEM((span, kv_width), jnp.bfloat16),
            pltpu.VMEM((tokens, span), jnp.float32),
            dma((shards, 2 * per_core)),
            dma((shards, 2 * per_core)),
            dma((shards, 2 * per_core)),
            dma((3, per_core)),
            dma((2, 2 * per_core)),
            dma((2, per_core)),
            dma((per_core,)),
            dma((shards, tiles)),
            dma((shards, tiles)),
        ],
        compiler_params=pltpu.CompilerParams(
            collective_id=0, has_side_effects=True, vmem_limit_bytes=60 * 1024 * 1024
        ),
        cost_estimate=pl.CostEstimate(
            flops=flops, bytes_accessed=8 * 1024 * 1024, transcendentals=heads * tokens * span
        ),
    )(queries, fresh_keys, fresh_values, key_pages, value_pages, table, lengths, weight)


def square_kernel(
    line, q_hbm, fk_hbm, fv_hbm, kp_hbm, vp_hbm, table_ref, len_ref, w_ref, out_ref,
    q_ref, kp_ref, vp_ref, act, wall, far_wall, relay, px_out, px_in, keep, stage, keys, values, bias,
    w_recv, w_swap, w_send, r_recv, own_sem, act_recv, act_send,
    px_recv, px_send, out_recv, out_send, in_sem,
    far_out, far_in, far_keep, far_stage, far_recv,
):
    group, dp, core = lax.axis_index("groups"), lax.axis_index("dp"), lax.axis_index("tensor")
    z, y = dp // 2, dp % 2
    x = group % 2
    cousin = group + 1 - 2 * x
    other = 1 - core
    half = z // 2
    inner = z % 2 != half
    outer = jnp.logical_not(inner)
    zp = z + 1 - 2 * (z % 2)
    zm = jnp.where(inner, line - 1 - z, z)
    peer = z * 2 + 1 - y
    part, cols = w_ref.shape
    tokens, wide = q_ref.shape
    chunks = part // CHUNK
    unit = cols // 2
    lane = unit // 2
    tall = 2 * CHUNK
    rows_mine = tokens // 2
    steps = wide // 256
    step_cols = wide // steps
    heads_per_step = step_cols // HEAD_SIZE
    near, far = steps * OUTER_ZY // 8, steps * INNER_ZY // 8

    def remote(src, dst, send, recv, where):
        return pltpu.make_async_remote_copy(
            src_ref=src, dst_ref=dst, send_sem=send, recv_sem=recv,
            device_id=where, device_id_type=pl.DeviceIdType.MESH,
        )

    def loop(low, high, act_on):
        lax.fori_loop(low, high, lambda k, carry: (act_on(k), carry)[1], 0)

    def rows(k):
        return pl.ds(pl.multiple_of(k * CHUNK, CHUNK), CHUNK)

    cached = table_ref.shape[1] * PAGE_TOKENS

    loads = [
        pltpu.make_async_copy(kp_hbm, kp_ref, in_sem.at[0]),
        pltpu.make_async_copy(vp_hbm, vp_ref, in_sem.at[1]),
        pltpu.make_async_copy(fk_hbm, keys.at[cached:], in_sem.at[2]),
        pltpu.make_async_copy(fv_hbm, values.at[cached:], in_sem.at[3]),
        pltpu.make_async_copy(q_hbm, q_ref, in_sem.at[4]),
    ]
    for copy in loads:
        copy.start()

    barrier = pltpu.get_barrier_semaphore()

    def greet(where):
        pl.semaphore_signal(barrier, inc=1, device_id=where, device_id_type=pl.DeviceIdType.MESH)

    greet((group, dp, other))
    for chip in (peer, zp * 2 + y):
        greet((group, chip, core))
        greet((group, chip, other))

    @pl.when(inner)
    def _():
        greet((cousin, dp, core))
        greet((group, zm * 2 + y, core))

    pl.semaphore_wait(barrier, 5 + jnp.where(inner, 2, 0))

    half_cols = pl.ds(pl.multiple_of(x * unit, 128), unit)
    half_lane = pl.ds(pl.multiple_of(x * lane, 128), lane)
    rest_cols = pl.ds(pl.multiple_of((1 - x) * unit, 128), unit)
    rest_lane = pl.ds(pl.multiple_of((1 - x) * lane, 128), lane)
    deep = chunks // 2
    pieces = deep + chunks

    def patch(k):
        if isinstance(k, jax.Array) or k < deep:
            return 0, pl.ds(pl.multiple_of(k * tall, tall), tall)
        return 1, pl.ds((k - deep) * CHUNK, CHUNK)

    def mid_own(k):
        return remote(
            w_ref.at[rows(k), half_cols], wall.at[1, rows(k), half_cols],
            w_send.at[0], w_recv.at[0, k], (group, zm * 2 + y, core),
        )

    def to_relay(k):
        v, part_rows = patch(k)
        column = pl.ds(pl.multiple_of(x * unit + v * lane, 128), lane)
        return remote(
            w_ref.at[part_rows, column], relay.at[v, part_rows],
            w_send.at[0], r_recv.at[k], (group, zp * 2 + y, core),
        )

    def mid_relay(k):
        v, part_rows = patch(k)
        return remote(
            relay.at[v, part_rows], far_wall.at[v, part_rows, half_lane],
            w_send.at[1], w_recv.at[1, k], (group, zm * 2 + y, core),
        )

    def slant(k):
        v, part_rows = patch(k)
        return remote(
            relay.at[v, part_rows], far_wall.at[v, part_rows, half_lane],
            w_send.at[3], w_swap.at[1 + v], (cousin, zm * 2 + y, core),
        )

    def side(s, k):
        if s == 1:
            ref, sem = wall.at[1, rows(k), half_cols], w_swap.at[0]
        else:
            v, part_rows = patch(k)
            ref, sem = far_wall.at[v, part_rows, half_lane], w_swap.at[1 + v]
        return remote(ref, ref, w_send.at[s + 1], sem, (cousin, dp, core))

    def swapped(ref, n):
        remote(ref, ref, w_send.at[2], w_swap.at[n], (cousin, dp, core)).wait_recv()

    def near_swapped():
        swapped(wall.at[1, :, rest_cols], 0)

    def far_swapped(v):
        swapped(far_wall.at[v, :, rest_lane], 1 + v)

    def relay_on(k):
        to_relay(k).wait_recv()
        mid_relay(k).start()

    def side_on(s, k):
        (mid_own(k) if s == 1 else mid_relay(k)).wait_recv()
        side(s, k).start()

    def own_copy():
        return pltpu.make_async_copy(w_ref, wall.at[0], own_sem.at[0])

    @pl.when(inner)
    def _():
        loop(0, chunks, lambda k: mid_own(k).start())

    @pl.when(outer)
    def _():
        to_relay(0).start()

    own_copy().start()

    length = len_ref[dp]
    position = lax.broadcasted_iota(jnp.int32, (tokens, cached), 1)
    bias[:, :cached] = jnp.where(position < length, 0.0, MASKED)
    bias[:, cached:] = jnp.where(
        lax.broadcasted_iota(jnp.int32, (tokens, tokens), 1)
        <= lax.broadcasted_iota(jnp.int32, (tokens, tokens), 0),
        0.0, MASKED,
    )
    for copy in loads:
        copy.wait()
    for j in range(table_ref.shape[1]):
        page = table_ref[0, j]
        keys[j * PAGE_TOKENS:(j + 1) * PAGE_TOKENS, :] = kp_ref[page]
        values[j * PAGE_TOKENS:(j + 1) * PAGE_TOKENS, :] = vp_ref[page]

    def act_at(slot, i):
        return act.at[slot, :, pl.ds(pl.multiple_of(i * step_cols, step_cols), step_cols)]

    def act_y(i):
        return remote(act_at(0, i), act_at(1, i), act_send.at[0], act_recv.at[1, i],
                      (group, peer, core))

    def act_z(i):
        return remote(act_at(0, i), act_at(2, i), act_send.at[1], act_recv.at[0, i],
                      (group, zp * 2 + y, core))

    def on_y(i):
        return remote(act_at(2, i), act_at(3, i), act_send.at[2], act_recv.at[1, steps],
                      (group, peer, core))

    def on_z(i):
        return remote(act_at(1, i), act_at(3, i), act_send.at[3], act_recv.at[1, steps],
                      (group, zp * 2 + y, core))

    over_y = steps - jnp.where(inner, near, far)
    over_z = steps - jnp.where(inner, far, near)

    def from_y(i):
        act_y(i).wait_recv()

        @pl.when(i < over_z)
        def _():
            on_z(i).start()

    def from_z(i):
        act_z(i).wait_recv()

        @pl.when(i >= over_y)
        def _():
            on_y(i).start()

    P = functools.partial

    def own_y(i):
        act_y(i).start()

    def attention_step(i):
        kv = (i * heads_per_step) // QUERY_GROUP
        kv_cols = pl.ds(pl.multiple_of(kv * HEAD_SIZE, HEAD_SIZE), HEAD_SIZE)
        for n in range(heads_per_step):
            start = pl.multiple_of((i * heads_per_step + n) * HEAD_SIZE, HEAD_SIZE)
            q = q_ref[:, pl.ds(start, HEAD_SIZE)]
            scores = lax.dot_general(
                q, keys[:, kv_cols], (((1,), (1,)), ((), ())), preferred_element_type=jnp.float32
            )
            scores = scores * SCALE + bias[...]
            weights = jnp.exp2(scores - jnp.max(scores, axis=-1, keepdims=True))
            total = jnp.sum(weights, axis=-1, keepdims=True)
            weighted = jnp.dot(
                weights.astype(jnp.bfloat16), values[:, kv_cols], preferred_element_type=jnp.float32
            )
            act[0, :, pl.ds(start, HEAD_SIZE)] = (weighted / total).astype(jnp.bfloat16)
        act_z(i).start()

        @pl.when(jnp.logical_or(outer, i < 2))
        def _():
            act_y(i).start()

        @pl.when(jnp.logical_and(outer, jnp.logical_and(i % 2 == 1, i < 2 * deep - 2)))
        def _():
            to_relay((i + 1) // 2).start()

        def at(n, *todo):
            @pl.when(jnp.logical_and(inner, i == n))
            def _():
                for act_now in todo:
                    act_now()

        at(3, P(side_on, 1, 0), P(relay_on, 0))
        at(4, P(from_z, 0), P(own_y, 2))
        at(5, P(side_on, 1, 1), P(from_y, 0))
        at(7, P(side_on, 1, 2), P(from_z, 1), P(own_y, 3))

    loop(0, steps, attention_step)

    @pl.when(outer)
    def _():
        for k in range(deep, pieces):
            to_relay(k).start()

    def shard_z(s):
        return jnp.where(s == 0, z, zm)

    def task(s, slot):
        return s * 4 + slot

    def swap(t):
        return remote(px_out.at[t], px_in.at[t], px_send.at[0], px_recv.at[t], (group, dp, other))

    my_rows = pl.ds(pl.multiple_of(core * rows_mine, rows_mine), rows_mine)
    mate_rows = pl.ds(pl.multiple_of(other * rows_mine, rows_mine), rows_mine)

    def place(s):
        zs = shard_z(s)
        to = zs // 2
        column = (zs * 2 + y - to * line) * cols
        return to, out_ref.at[my_rows, pl.ds(pl.multiple_of(column, 128), cols)]

    def owner(slot):
        return jnp.where(slot >= 2, zp, z) * 2 + jnp.where(slot % 2 == 1, 1 - y, y)

    def stays(s, slot):
        return jnp.logical_and(slot == 0, shard_z(s) // 2 == core)

    def begin(s, slot):
        t = task(s, slot)
        keep[t] = jnp.dot(act[slot], wall[s], preferred_element_type=jnp.float32)
        px_out[t] = keep[t, mate_rows, :].astype(jnp.bfloat16)
        swap(t).start()

    def finish(s, slot):
        t = task(s, slot)
        swap(t).wait_recv()
        stage[t] = (keep[t, my_rows, :] + px_in[t].astype(jnp.float32)).astype(jnp.bfloat16)
        to, ref = place(s)

        @pl.when(stays(s, slot))
        def _():
            pltpu.make_async_copy(stage.at[t], ref, out_recv.at[0]).start()

        @pl.when(jnp.logical_not(stays(s, slot)))
        def _():
            remote(stage.at[t], ref, out_send.at[0], out_recv.at[0], (group, owner(slot), to)).start()

    def half_swap(p, h):
        pair = pl.ds(p * 2, 2)
        column = pl.ds(pl.multiple_of(h * lane, 128), lane)
        return remote(far_out.at[1, pair, :, column], far_in.at[1, pair, :, column], px_send.at[1],
                      far_recv.at[1 + h, p], (group, dp, other))

    def half_begin(p, h):
        pair = pl.ds(p * 2, 2)
        column = pl.ds(pl.multiple_of(h * lane, 128), lane)
        far_keep[1, pair, :, column] = jnp.dot(
            act[pair].reshape(2 * tokens, wide), far_wall[1, :, column], preferred_element_type=jnp.float32,
        ).reshape(2, tokens, lane)
        far_out[1, pair, :, column] = far_keep[1, pair, mate_rows, column].astype(jnp.bfloat16)
        half_swap(p, h).start()

    def half_finish(p, h):
        half_swap(p, h).wait_recv()
        pair = pl.ds(p * 2, 2)
        column = pl.ds(pl.multiple_of(h * lane, 128), lane)
        far_stage[1, pair, :, column] = (
            far_keep[1, pair, my_rows, column] + far_in[1, pair, :, column].astype(jnp.float32)
        ).astype(jnp.bfloat16)
        far_send(1, p, h)

    def far_swap(v, p):
        pair = pl.ds(p * 2, 2)
        return remote(far_out.at[v, pair], far_in.at[v, pair], px_send.at[1], far_recv.at[v, p],
                      (group, dp, other))

    def far_begin(v, p):
        pair = pl.ds(p * 2, 2)
        far_keep[v, pair] = jnp.dot(
            act[pair].reshape(2 * tokens, wide), far_wall[v], preferred_element_type=jnp.float32,
        ).reshape(2, tokens, unit)
        far_out[v, pair] = far_keep[v, pair, mate_rows, :].astype(jnp.bfloat16)
        far_swap(v, p).start()

    def far_stays(slot):
        return jnp.logical_and(slot == 0, 1 - half == core)

    def far_finish(v, p):
        far_swap(v, p).wait_recv()
        pair = pl.ds(p * 2, 2)
        far_stage[v, pair] = (
            far_keep[v, pair, my_rows, :] + far_in[v, pair].astype(jnp.float32)
        ).astype(jnp.bfloat16)
        far_send(v, p, 0)
        far_send(v, p, 1)

    def far_send(v, p, h):
        zs = (line - 1) * (1 - half)
        to = zs // 2
        column = (zs * 2 + y - to * line) * cols + h * unit + v * lane
        ref = out_ref.at[my_rows, pl.ds(pl.multiple_of(column, 128), lane)]

        def tile(slot):
            return far_stage.at[v, slot, :, pl.ds(pl.multiple_of(h * lane, 128), lane)]

        def go(slot):
            remote(tile(slot), ref, out_send.at[1], out_recv.at[0], (group, owner(slot), to)).start()

        go(p * 2 + 1)

        @pl.when(far_stays(p * 2))
        def _():
            pltpu.make_async_copy(tile(p * 2), ref, out_recv.at[0]).start()

        @pl.when(jnp.logical_not(far_stays(p * 2)))
        def _():
            go(p * 2)

    own_copy().wait()

    def run(count, kinds, duties, prompt):
        def each(n, what):
            for holds, which, acts in kinds:
                @pl.when(holds(n))
                def _():
                    acts[what](*which(n))

        def one(n):
            early = functools.reduce(jnp.logical_or, [n == m + 1 for m in prompt])

            for at, todo in duties.items():
                @pl.when(n == at)
                def _():
                    for act_now in todo:
                        act_now()

            @pl.when(n < count)
            def _():
                each(n, 0)

            @pl.when(jnp.logical_and(n > 0, jnp.logical_not(early)))
            def _():
                each(n - 1, 1)

        loop(0, count + 1, one)

    def corner_landed():
        remote(act.at[2], act.at[3], act_send.at[2], act_recv.at[1, steps], (group, peer, core)).wait_recv()

    near_tasks = (begin, finish)
    far_tasks = (far_begin, far_finish)
    half_tasks = (half_begin, half_finish)

    @pl.when(outer)
    def _():
        run(4, [(lambda n: n >= 0, lambda n: (0, n), near_tasks)], {
            1: [P(finish, 0, 0), lambda: loop(0, steps, from_z), lambda: loop(0, steps, from_y)],
            3: [P(finish, 0, 2), corner_landed],
        }, (0, 2))

    @pl.when(inner)
    def _():
        def is_far(n):
            return jnp.logical_or(n == 9, n == 6)

        def is_half(n):
            return n >= 10

        def near_which(n):
            m = jnp.where(n < 7, n, n - 1)
            group = m // 2
            return m % 2, jnp.where(group == 0, 0, jnp.where(group == 3, 1, group + 1))

        def far_which(n):
            return 0, jnp.where(n == 6, 1, 0)

        def half_which(n):
            return 1 - n % 2, jnp.where(n < 12, x, 1 - x)

        last = pieces - 1
        kinds = [
            (lambda n: jnp.logical_not(jnp.logical_or(is_far(n), is_half(n))), near_which, near_tasks),
            (is_far, far_which, far_tasks), (is_half, half_which, half_tasks),
        ]
        run(14, kinds, {
            0: [P(side_on, 1, 3), P(relay_on, 1), P(from_y, 1)],
            1: [P(side_on, 1, 4), P(from_z, 2), P(from_y, 2), P(finish, 0, 0), P(side_on, 1, 5), P(from_z, 3), P(own_y, 4),
                P(side_on, 1, 6), P(relay_on, 2), P(side_on, 1, 7), P(from_z, 4), P(from_z, 5), P(own_y, 5),
                P(side_on, 2, 0), P(relay_on, 3), P(side_on, 2, 1), near_swapped],
            2: [P(from_z, 6), P(side_on, 2, 2), P(from_z, 7), P(own_y, 6), P(own_y, 7)],
            3: [P(relay_on, 4), P(side_on, 2, 3)],
            4: [P(relay_on, 5), P(relay_on, 6), P(finish, 1, 2), P(side_on, 2, 4), P(relay_on, 7), P(side_on, 2, 5),
                P(relay_on, 8), corner_landed],
            5: [P(side_on, 2, 6), P(relay_on, 9)],
            6: [P(side_on, 2, 7), P(relay_on, 10), P(far_swapped, 0)],
            7: [P(side_on, 2, 8), P(relay_on, last), slant(last).start, P(side_on, 2, 9), lambda: loop(3, steps, from_y)],
            9: [P(side_on, 2, 10)],
            10: [mid_relay(last).wait_recv],
            12: [P(half_finish, 0, x), P(far_swapped, 1)],
        }, (0, 3, 11))

    def sent(ref, sem):
        remote(ref, ref, sem, sem, (group, dp, other)).wait_send()

    def sent_if(holds, ref, sem):
        @pl.when(holds)
        def _():
            sent(ref, sem)

    sent(act.at[0], act_send.at[0])
    sent(act.at[0], act_send.at[1])
    unit_ref = wall.at[0, :, 0:unit]
    sent(unit_ref, w_send.at[0])
    far_goes = jnp.logical_and(inner, core == half)
    far_mate = jnp.logical_and(inner, core != half)
    sent_if(inner, stage.at[0:7], out_send.at[0])
    sent_if(jnp.logical_and(outer, core == half), stage.at[0:3], out_send.at[0])
    sent_if(jnp.logical_and(outer, core != half), stage.at[0:4], out_send.at[0])
    sent_if(inner, px_out, px_send.at[0])
    sent_if(outer, px_out.at[0:4], px_send.at[0])
    sent_if(inner, far_out, px_send.at[1])
    sent_if(far_goes, far_stage, out_send.at[1])
    sent_if(far_mate, far_stage.at[:, 0:3], out_send.at[1])
    for n in range(1, 4):
        sent_if(inner, unit_ref, w_send.at[n])

    def columns(low, high):
        return act.at[0, :, low * step_cols:high * step_cols]

    for holds, y_count, z_count in ((inner, near, steps - far), (outer, far, steps - near)):
        if y_count:
            sent_if(holds, columns(0, y_count), act_send.at[2])
        if z_count:
            sent_if(holds, columns(0, z_count), act_send.at[3])

    remote(out_ref, out_ref, out_recv.at[0], out_recv.at[0], (group, dp, other)).wait_recv()


def square_program(line, queries, fresh_keys, fresh_values, key_pages, value_pages, table, lengths, weight):
    tokens, wide = queries.shape
    part, cols = weight.shape
    chunks = part // CHUNK
    steps = wide // 256
    unit = cols // 2
    span = table.shape[1] * PAGE_TOKENS + tokens
    kv_width = fresh_keys.shape[1]
    hbm = pl.BlockSpec(memory_space=pl.ANY)
    smem = pl.BlockSpec(memory_space=pltpu.SMEM)
    dma = pltpu.SemaphoreType.DMA
    bf16, f32 = jnp.bfloat16, jnp.float32
    heads = wide // HEAD_SIZE
    flops = 4 * heads * tokens * span * HEAD_SIZE + 2 * 24 * tokens * part * unit
    return pl.pallas_call(
        functools.partial(square_kernel, line),
        out_shape=jax.ShapeDtypeStruct((tokens, line * cols), bf16),
        in_specs=[hbm, hbm, hbm, hbm, hbm, smem, smem, hbm],
        out_specs=hbm,
        scratch_shapes=[
            pltpu.VMEM(queries.shape, bf16),
            pltpu.VMEM(key_pages.shape, bf16),
            pltpu.VMEM(value_pages.shape, bf16),
            pltpu.VMEM((4, tokens, wide), bf16),
            pltpu.VMEM((2, part, cols), bf16),
            pltpu.VMEM((2, part, unit), bf16),
            pltpu.VMEM((2, part, unit // 2), bf16),
            pltpu.VMEM((8, tokens // 2, cols), bf16),
            pltpu.VMEM((8, tokens // 2, cols), bf16),
            pltpu.VMEM((8, tokens, cols), f32),
            pltpu.VMEM((8, tokens // 2, cols), bf16),
            pltpu.VMEM((span, kv_width), bf16),
            pltpu.VMEM((span, kv_width), bf16),
            pltpu.VMEM((tokens, span), f32),
            dma((2, chunks + chunks // 2)),
            dma((3,)),
            dma((4,)),
            dma((chunks + chunks // 2,)),
            dma((1,)),
            dma((2, steps + 1)),
            dma((4,)),
            dma((8,)),
            dma((2,)),
            dma((1,)),
            dma((2,)),
            dma((5,)),
            pltpu.VMEM((2, 4, tokens // 2, unit), bf16),
            pltpu.VMEM((2, 4, tokens // 2, unit), bf16),
            pltpu.VMEM((2, 4, tokens, unit), f32),
            pltpu.VMEM((2, 4, tokens // 2, unit), bf16),
            dma((3, 2)),
        ],
        compiler_params=pltpu.CompilerParams(
            collective_id=0, has_side_effects=True, vmem_limit_bytes=60 * 1024 * 1024
        ),
        cost_estimate=pl.CostEstimate(
            flops=flops, bytes_accessed=8 * 1024 * 1024, transcendentals=heads * tokens * span
        ),
    )(queries, fresh_keys, fresh_values, key_pages, value_pages, table, lengths, weight)


def program_of(line):
    return square_program if line == 4 else shards_program


def solution(mesh):
    return jax.shard_map(
        functools.partial(program_of(mesh.shape["dp"] // 2), mesh.shape["dp"] // 2),
        mesh=mesh,
        in_specs=(
            P(("groups", "dp"), "tensor"),
            P(("groups", "dp"), "tensor"),
            P(("groups", "dp"), "tensor"),
            P(("groups", "dp"), None, "tensor"),
            P(("groups", "dp"), None, "tensor"),
            P(("groups", "dp"), None),
            P("groups"),
            P("tensor", "dp"),
        ),
        out_specs=P(("groups", "dp"), "tensor"),
        check_vma=False,
    )
```
